256 devices in a mesh: dp: 8 (over x, core), expert: 32 (over y, z).
Axes of the slice: x: 4, y: 4, z: 8, core: 2. Of those that a mesh axis runs over, the one named last changes fastest.
Arguments:
- tokens: bfloat16 [4096, 4096], P(('dp', 'expert')), may hold values from -6 to 6
- routes: int32 [4096, 8], P(('dp', 'expert')), may hold values from 0 to 127, all different within a row; in each aligned block of 16 rows (0 to 15, 16 to 31, ...) at most 2 rows name the same one
- route_gates: float32 [4096, 8], P(('dp', 'expert')), may hold values from 0.02 to 0.5
- placement: int32 [128], replicated, may hold values from 0 to 127, each once
- swap_flags: int32 [128], replicated, may hold values from 0 to 1, as said below
- gate_weight: bfloat16 [32, 4096, 3072], P('expert', None, 'dp'), may hold values from -0.09375 to 0.09375
- up_weight: bfloat16 [32, 4096, 3072], P('expert', None, 'dp'), may hold values from -0.09375 to 0.09375
- down_weight: bfloat16 [32, 3072, 4096], P('expert', 'dp'), may hold values from -0.21875 to 0.21875
Outputs:
- layer_out: bfloat16 [4096, 4096], P(('dp', 'expert'))
The draws below stay inside these ranges and needn't reach their ends.
Inputs may be any that keep to these rules, and one draw needn't show every extreme that they name: `routes`: each row names 8 different experts; among the 16 rows of one device no expert is named more than 2 times, a bound that some block reaches. `placement`: A permutation of the 128 positions. swap_flags[P] equals swap_flags[(P + 64) mod 128].
All inputs are finite; a program needn't handle non-finite values.
Results may differ from the reference program's by a relative error of at most 0.0065.
Values may be sent and summed in bfloat16 or wider, within the bound.
A program may use at most 128 MiB of HBM per device.

```python
import math
import jax
import jax.numpy as jnp
import numpy as np
from jax import lax

D = 4096
FF = 768
TOP = 8
TOK_DEV = 16
SLOTS = 4
EXPERTS = 128
MOST = 2
TOKENS = 4096
N_DP = 8
N_EXPERT = 32


def draw_swap_flags(key, part):
    pair_bits = jax.random.randint(key, (EXPERTS // 2,), 0, 2, dtype=jnp.int32)
    return jnp.concatenate([pair_bits, pair_bits])


def levels(stream_key, shape, split, low, top_value):
    def one(dim, parts):
        heights = jax.random.uniform(jax.random.fold_in(jax.random.fold_in(stream_key, 6), dim), (parts,), jnp.float32, low / len(split), top_value / len(split))
        return jnp.repeat(jnp.exp(heights), shape[dim] // parts).reshape((-1,) + (1,) * (len(shape) - dim - 1))

    factor_of = one(*split[0])
    for cut in split[1:]:
        factor_of = factor_of * one(*cut)
    return factor_of


def assign_block(own_key, own, number, rows, amount, top, limit, slope):
    order = jax.random.permutation(own_key, amount)
    crowded, common = shares(amount, rows * top, limit, slope, True), shares(amount, rows * top, limit, slope, False)
    places = jnp.arange(amount)

    def named(tallies, turn):
        used = int((tallies > 0).sum())
        fixed = max(1, used // 4)
        moved = fixed + (places - fixed + turn * (used - fixed)) % max(1, amount - fixed)
        return jnp.zeros((amount,), jnp.int32).at[order[jnp.where(places < fixed, places, moved)]].set(jnp.asarray(tallies, jnp.int32))

    tallies = jnp.where(number % 4 == 0, named(crowded, number // 4), named(common, number - number // 4 - 1))
    mixed = jax.random.permutation(jax.random.fold_in(own, 3), amount)
    donor, sink = mixed[0:amount // 2 * 2:2], mixed[1:amount // 2 * 2:2]
    slack = jnp.minimum(tallies[donor] - 1, limit - tallies[sink]) // 2
    slack = jnp.where((donor == order[0]) | (sink == order[0]) | (tallies[sink] == 0), 0, jnp.maximum(slack, 0))
    moved = jax.random.randint(jax.random.fold_in(own, 4), (amount // 2,), 0, 1 << 20) % (slack + 1)
    tallies = tallies.at[donor].add(-moved).at[sink].add(moved)
    labels = jnp.searchsorted(jnp.cumsum(tallies), jnp.arange(rows * top), side="right").astype(jnp.int32)
    grid = labels.reshape(top, rows).T
    grid = grid[jax.random.permutation(jax.random.fold_in(own, 1), rows)]
    turn = jax.random.randint(jax.random.fold_in(own, 2), (rows, 1), 0, top)
    return jnp.take_along_axis(grid, (jnp.arange(top)[None, :] + turn) % top, axis=1)


def shares(amount, total, limit, skew, full):
    loads = [(1 << 20) // math.isqrt(rank ** skew) + 1 for rank in range(1, amount + 1)]
    largest = limit if full else min(limit, max(-(-total // amount), total * loads[0] // sum(loads)))
    least = 1 if total - largest >= amount - 1 else 0
    counts, spare = [largest] + [least] * (amount - 1), total - largest - least * (amount - 1)
    while spare > 0:
        candidates = [i for i in range(1, amount) if counts[i] < largest] or [i for i in range(1, amount) if counts[i] < limit]
        mass, budget = sum([loads[i] for i in candidates]), spare
        for i in candidates:
            addition = min(limit - counts[i], max(1, budget * loads[i] // mass), spare)
            counts[i] = counts[i] + addition
            spare = spare - addition
    return np.array(counts)


def normal_values(own_key, dims, scale, reach, split=(), kind=jnp.bfloat16):
    level = levels(own_key, dims, split, -0.22, 0.18) if split else 1.0
    result = jax.random.normal(own_key, dims, jnp.float32) * scale * level
    return jnp.minimum(jnp.maximum(result, -reach), reach).astype(kind)


def setup_inputs(seed: int = 0) -> dict:
    arg_keys = jax.random.split(jax.random.key(seed), 9)
    tokens = normal_values(arg_keys[0], (TOKENS, D), 1.0, 6.0, ((0, 256),))
    routes_keys = jax.random.split(jax.random.fold_in(arg_keys[1], 1), TOKENS // TOK_DEV)
    routes_turns = jax.random.permutation(jax.random.fold_in(arg_keys[1], 3), TOKENS // TOK_DEV)
    routes = jax.vmap(lambda own, number: assign_block(jax.random.fold_in(arg_keys[1], 2), own, number, TOK_DEV, EXPERTS, TOP, MOST, 3))(routes_keys, routes_turns).reshape((TOKENS, TOP))
    route_gates = jnp.clip(jnp.exp(math.log(0.5) - 3.218876 * jax.random.uniform(arg_keys[2], (TOKENS, TOP), jnp.float32) ** levels(arg_keys[2], (TOKENS, TOP), ((0, 256),), -0.2, 0.2)), 0.02, 0.5)
    placement = jax.random.permutation(arg_keys[3], EXPERTS).astype(jnp.int32)
    swap_flags = draw_swap_flags(jax.random.fold_in(arg_keys[8], 71), 0)
    gate_weight = normal_values(arg_keys[5], (N_EXPERT, D, SLOTS * FF), D ** -0.5, 0.09375, ((0, 32), (2, 8)))
    up_weight = normal_values(arg_keys[6], (N_EXPERT, D, SLOTS * FF), D ** -0.5, 0.09375, ((0, 32), (2, 8)))
    down_weight = normal_values(arg_keys[7], (N_EXPERT, SLOTS * FF, D), FF ** -0.5, 0.21875, ((0, 32), (1, 8)))
    return dict(tokens=tokens, routes=routes, route_gates=route_gates, placement=placement, swap_flags=swap_flags, gate_weight=gate_weight, up_weight=up_weight, down_weight=down_weight)


def reference(tokens, routes, route_gates, placement, swap_flags, gate_weight, up_weight, down_weight):
    experts = placement.shape[0]
    slot_count = experts // N_EXPERT
    half_width = FF // 2
    capacity = N_DP * N_EXPERT * MOST
    flags_at = swap_flags[placement]
    holder = jnp.where(flags_at == 1, (placement + experts // 2) % experts, placement).astype(jnp.int32)

    def per_expert(accum_out, expert_id):
        matches = routes == expert_id
        gate_row = jnp.sum(jnp.where(matches, route_gates, jnp.float32(0.0)), axis=1)
        chosen = jnp.any(matches, axis=1)
        picked_rows = jnp.nonzero(chosen, size=capacity, fill_value=0)[0].astype(jnp.int32)
        valid = (jnp.arange(capacity, dtype=jnp.int32) < jnp.sum(chosen.astype(jnp.int32))).astype(jnp.float32)
        received = tokens[picked_rows].astype(jnp.float32)
        position = holder[expert_id]
        column = (position // slot_count).astype(jnp.int32)
        slot_id = (position % slot_count).astype(jnp.int32)
        start = (slot_id * FF).astype(jnp.int32)
        zero = jnp.int32(0)
        block_gate = lax.dynamic_slice(gate_weight, (column, zero, start), (1, D, FF))[0]
        block_up = lax.dynamic_slice(up_weight, (column, zero, start), (1, D, FF))[0]
        block_down = lax.dynamic_slice(down_weight, (column, start, zero), (1, FF, D))[0]
        expert_sum = jnp.zeros((capacity, D), jnp.float32)
        for half_id in range(2):
            lower = half_id * half_width
            upper = lower + half_width
            gate_act = jnp.dot(received, block_gate[:, lower:upper].astype(jnp.float32), precision=lax.Precision.HIGHEST)
            up_act = jnp.dot(received, block_up[:, lower:upper].astype(jnp.float32), precision=lax.Precision.HIGHEST)
            hidden = (jax.nn.silu(gate_act) * up_act).astype(jnp.bfloat16)
            hidden = lax.optimization_barrier(hidden).astype(jnp.float32)
            partial_value = jnp.dot(hidden, block_down[lower:upper, :].astype(jnp.float32), precision=lax.Precision.HIGHEST).astype(jnp.bfloat16)
            partial_value = lax.optimization_barrier(partial_value).astype(jnp.float32)
            expert_sum = expert_sum + partial_value
        expert_rows = lax.optimization_barrier(expert_sum.astype(jnp.bfloat16)).astype(jnp.float32)
        scale = gate_row[picked_rows] * valid
        accum_out = accum_out.at[picked_rows].add(expert_rows * scale[:, None])
        return accum_out, None

    start_out = jnp.zeros((TOKENS, D), jnp.float32)
    final_out, unused = lax.scan(per_expert, start_out, jnp.arange(experts, dtype=jnp.int32))
    return final_out.astype(jnp.bfloat16)
```

```python
import functools

import jax
import jax.numpy as jnp
from jax import lax
from jax.experimental import pallas as pl
from jax.experimental.pallas import tpu as pltpu
from jax.sharding import PartitionSpec as P

NX, NY, NZ = 4, 4, 8
PLANE = NX * NY
ROWS = 16
WIDE = 4096
HALF = 384
CHUNKS = 4
CW = WIDE // CHUNKS
TILE = 256
MESH = pl.DeviceIdType.MESH
F32 = jnp.float32
BF16 = jnp.bfloat16


def dot(a, b):
    return jnp.dot(a, b, preferred_element_type=F32)


def kernel(
    tokens, routes, gates, placement, flags, w_gate, w_up, w_down, out,
    tok, meta, sel, comb, comb_t, away, rows, w_in, w_out, acc, hid,
    mine, theirs, got, ret, back, part, hop_out, hop_in,
    w_sem, meta_send, meta_recv, ag_send, ag_recv, go_send, go_recv, sib_send, sib_recv,
    half_send, half_recv, back_send, back_recv, rs_send, rs_recv,
):
    dp = lax.axis_index("dp")
    ex = lax.axis_index("expert")
    x, core = dp // 2, dp % 2
    y, z = ex // NZ, ex % NZ
    sibling = (x * 2 + (1 - core), ex)

    def along_z(by):
        return (dp, y * NZ + (z + by + NZ) % NZ)

    def in_plane(dx, dy):
        return (((x + dx + NX) % NX) * 2 + core, ((y + dy + NY) % NY) * NZ + z)

    def remote(src, dst, send, recv, device):
        return pltpu.make_async_remote_copy(
            src_ref=src, dst_ref=dst, send_sem=send, recv_sem=recv, device_id=device, device_id_type=MESH
        )

    barrier = pltpu.get_barrier_semaphore()
    for i in range(1, NZ):
        pl.semaphore_signal(barrier, inc=1, device_id=along_z(i), device_id_type=MESH)
    for d in range(1, PLANE):
        pl.semaphore_signal(barrier, inc=1, device_id=in_plane(d % NX, d // NX), device_id_type=MESH)
    pl.semaphore_signal(barrier, inc=1, device_id=sibling, device_id_type=MESH)

    loads = (
        pltpu.make_async_copy(w_gate.at[0], w_in.at[:, pl.ds(0, HALF)], w_sem.at[0]),
        pltpu.make_async_copy(w_up.at[0], w_in.at[:, pl.ds(HALF, HALF)], w_sem.at[1]),
        pltpu.make_async_copy(w_down.at[0], w_out, w_sem.at[2]),
    )
    for load in loads:
        load.start()

    for c in range(CHUNKS):
        tok[c, 0] = tokens[:, c * CW:(c + 1) * CW]
    meta[0] = jnp.zeros((ROWS, 128), F32)
    meta[0, :, 0:8] = routes[...].astype(F32)
    meta[0, :, 8:16] = gates[...]

    pl.semaphore_wait(barrier, NZ - 1 + PLANE - 1 + 1)

    meta_copies = [
        remote(meta.at[0], meta.at[i], meta_send.at[i], meta_recv.at[i], along_z(-i)) for i in range(1, NZ)
    ]
    for copy in meta_copies:
        copy.start()

    def ag(c, src, dst):
        by = -1 if src < dst else 1
        return remote(tok.at[c, src % NZ], tok.at[c, dst], ag_send.at[c, dst], ag_recv.at[c, dst], along_z(by))

    def ag_steps(c):
        down, up = (4, 3) if c % 2 == 0 else (3, 4)
        return [(i - 1, i) for i in range(1, down + 1)], [(NZ - i + 1, NZ - i) for i in range(1, up + 1)]

    started = {}

    def ag_start(c, src, dst):
        started[(c, dst)] = ag(c, src, dst)
        started[(c, dst)].start()

    for c in range(CHUNKS):
        for way in ag_steps(c):
            ag_start(c, *way[0])

    lane = lax.broadcasted_iota(jnp.int32, (128, 128), 1)
    line = lax.broadcasted_iota(jnp.int32, (128, 128), 0)
    lane_f = lane.astype(F32)
    placed = jnp.broadcast_to(placement[...].astype(F32), (128, 128)).T
    flag = jnp.sum(
        jnp.where(placed == lane_f, jnp.broadcast_to(flags[...].astype(F32), (128, 128)), 0.0), axis=1, keepdims=True
    )
    holder = jnp.where(flag == 0.0, placed, jnp.where(placed >= 64.0, placed - 64.0, placed + 64.0))
    offset = lane & (PLANE - 1)
    spot = ((((offset >> 2) + y) & (NY - 1)) * NZ + z) * NX + ((offset + x) & (NX - 1))
    where_to = jnp.where((holder == spot.astype(F32)) & (lane < 2 * PLANE), 1.0, 0.0).astype(BF16)

    for copy in meta_copies:
        copy.wait_recv()
    info = meta[...].reshape(NZ * ROWS, 128)
    named = jnp.zeros((128, 128), F32)
    weight = jnp.zeros((128, 128), F32)
    for k in range(8):
        hit = info[:, k:k + 1] == lane_f
        named = named + jnp.where(hit, 1.0, 0.0)
        weight = weight + jnp.where(hit, info[:, 8 + k:9 + k], 0.0)
    at = dot(named.astype(BF16), where_to)
    before = jnp.where(((line >> 4) == (lane >> 4)) & (lane < line), 1.0, 0.0).astype(BF16)
    rank = dot(before, at.astype(BF16))
    pick = jnp.where(rank == (lane >> 4).astype(F32), at, 0.0)
    high = weight.astype(BF16)
    low = (weight - high.astype(F32)).astype(BF16)
    tables = (pick.T, (dot(high, where_to) * pick).T, (dot(low, where_to) * pick).T)
    own = lax.broadcasted_iota(jnp.int32, (NZ, 128), 0) == (lax.broadcasted_iota(jnp.int32, (NZ, 128), 1) >> 4)
    for r in range(2):
        for t, table in enumerate(tables):
            spread = jnp.where(own[None], table[r * PLANE:(r + 1) * PLANE][:, None, :], 0.0)
            if t == 0:
                sel[:, r] = spread
            else:
                comb[t - 1, :, r] = spread
    chosen = sel[...].reshape(256, 128).astype(BF16)
    for t in range(2):
        flat = comb[t].reshape(256, 128)
        comb_t[pl.ds(t * 128, 128), 0:128] = flat[0:128].T.astype(BF16)
        comb_t[pl.ds(t * 128, 128), 128:256] = flat[128:256].T.astype(BF16)

    for s in range(1, 4):
        for c in range(CHUNKS):
            for way in ag_steps(c):
                if s < len(way):
                    started[(c, way[s - 1][1])].wait_recv()
                    ag_start(c, *way[s])

    def go(c, d):
        return remote(away.at[c, d], rows.at[c, 0, d], go_send.at[c], go_recv.at[c], in_plane(d % NX, d // NX))

    def go_all(c):
        return remote(away.at[c, pl.ds(1, PLANE - 1)], rows.at[c, 0, pl.ds(1, PLANE - 1)], go_send.at[c], go_recv.at[c], sibling)

    for c in range(CHUNKS):
        for way in ag_steps(c):
            started[(c, way[-1][1])].wait_recv()
            if len(way) == 3:
                pass
        block = tok[c].reshape(NZ * ROWS, CW)
        for n in range(0, CW, TILE):
            piece = dot(chosen, block[:, n:n + TILE]).astype(BF16).reshape(PLANE, ROWS, TILE)
            away[c, :, :, n:n + TILE] = piece
        rows[c, 0, 0] = away[c, 0]
        for d in range(1, PLANE):
            go(c, d).start()

    for load in loads[:2]:
        load.wait()

    def share(c):
        return remote(rows.at[c, 0], rows.at[c, 1], sib_send.at[c], sib_recv.at[c], sibling)

    def first(c, side):
        block = rows[c, side].reshape(256, CW)
        for n in range(0, 2 * HALF, TILE):
            term = dot(block, w_in[c * CW:(c + 1) * CW, n:n + TILE])
            at_rows = pl.ds(side * 256, 256)
            if c == 0:
                acc[at_rows, n:n + TILE] = term
            else:
                acc[at_rows, n:n + TILE] += term

    for c in range(CHUNKS):
        go_all(c).wait_recv()
        share(c).start()
        first(c, 0)
        if c > 0:
            share(c - 1).wait_recv()
            first(c - 1, 1)
    share(CHUNKS - 1).wait_recv()
    first(CHUNKS - 1, 1)

    gate_act = acc[:, 0:HALF]
    hid[...] = (gate_act / (1.0 + jnp.exp(-gate_act)) * acc[:, HALF:2 * HALF]).astype(BF16)
    loads[2].wait()

    def pair(c):
        return remote(theirs.at[c], got.at[c], half_send.at[c], half_recv.at[c], sibling)

    for c in range(CHUNKS):
        for n in range(0, CW, TILE):
            theirs[c, :, n:n + TILE] = dot(hid[256:512], w_out[:, c * CW + n:c * CW + n + TILE]).astype(BF16)
        pair(c).start()
        for n in range(0, CW, TILE):
            mine[c, :, n:n + TILE] = dot(hid[0:256], w_out[:, c * CW + n:c * CW + n + TILE]).astype(BF16)

    def home(c, d):
        return remote(ret.at[c, d], back.at[c, d], back_send.at[c], back_recv.at[c], in_plane(-(d % NX), -(d // NX)))

    def home_all(c):
        return remote(ret.at[c, pl.ds(1, PLANE - 1)], back.at[c, pl.ds(1, PLANE - 1)], back_send.at[c], back_recv.at[c], sibling)

    for c in range(CHUNKS):
        pair(c).wait_recv()
        both = (mine[c].astype(F32) + got[c].astype(F32)).astype(BF16)
        ret[c] = both.reshape(PLANE, ROWS, CW)
        back[c, 0] = ret[c, 0]
        for d in range(1, PLANE):
            home(c, d).start()

    def rs_steps(c):
        up, down = (4, 4 + 1) if c % 2 == 0 else (3, 4)
        return [(i, i - 1) for i in range(up, 0, -1)], [(i, i + 1) for i in range(down, NZ)]

    def rs(c, src, dst):
        by = 1 if dst < src else -1
        return remote(hop_out.at[c, src], hop_in.at[c, dst], rs_send.at[c, src], rs_recv.at[c, dst], along_z(by))

    for tick in range(CHUNKS + 4):
        if tick < CHUNKS:
            c = tick
            home_all(c).wait_recv()
            block = back[c].reshape(256, CW)
            for n in range(0, CW, TILE):
                two = dot(comb_t[...], block[:, n:n + TILE])
                part[c, :, :, n:n + TILE] = (two[0:128] + two[128:256]).reshape(NZ, ROWS, TILE)
            for way in rs_steps(c):
                src, dst = way[0]
                hop_out[c, src] = part[c, src].astype(BF16)
                rs(c, src, dst).start()
        for c in range(max(0, tick - 4), min(tick, CHUNKS)):
            step = tick - c
            for way in rs_steps(c):
                if step < len(way):
                    src, dst = way[step]
                    rs(c, *way[step - 1]).wait_recv()
                    hop_out[c, src] = (part[c, src] + hop_in[c, src].astype(F32)).astype(BF16)
                    rs(c, src, dst).start()
                elif step == len(way):
                    rs(c, *way[step - 1]).wait_recv()
            if step == 4:
                total = part[c, 0] + hop_in[c, 0].astype(F32) + hop_in[c, NZ].astype(F32)
                out[:, c * CW:(c + 1) * CW] = total.astype(BF16)

    for copy in meta_copies:
        copy.wait_send()
    for copy in started.values():
        copy.wait_send()
    for c in range(CHUNKS):
        go_all(c).wait_send()
        share(c).wait_send()
        pair(c).wait_send()
        home_all(c).wait_send()
        for way in rs_steps(c):
            for step in way:
                rs(c, *step).wait_send()


def on_device(tokens, routes, route_gates, placement, swap_flags, gate_weight, up_weight, down_weight):
    vmem = pl.BlockSpec(memory_space=pltpu.VMEM)
    hbm = pl.BlockSpec(memory_space=pl.ANY)
    dma = pltpu.SemaphoreType.DMA
    return pl.pallas_call(
        kernel,
        out_shape=jax.ShapeDtypeStruct(tokens.shape, tokens.dtype),
        in_specs=[vmem] * 5 + [hbm] * 3,
        out_specs=vmem,
        scratch_shapes=[
            pltpu.VMEM((CHUNKS, NZ, ROWS, CW), BF16),
            pltpu.VMEM((NZ, ROWS, 128), F32),
            pltpu.VMEM((PLANE, 2, NZ, 128), F32),
            pltpu.VMEM((2, PLANE, 2, NZ, 128), F32),
            pltpu.VMEM((256, 256), BF16),
            pltpu.VMEM((CHUNKS, PLANE, ROWS, CW), BF16),
            pltpu.VMEM((CHUNKS, 2, PLANE, ROWS, CW), BF16),
            pltpu.VMEM((WIDE, 2 * HALF), BF16),
            pltpu.VMEM((HALF, WIDE), BF16),
            pltpu.VMEM((512, 2 * HALF), F32),
            pltpu.VMEM((512, HALF), BF16),
            pltpu.VMEM((CHUNKS, 256, CW), BF16),
            pltpu.VMEM((CHUNKS, 256, CW), BF16),
            pltpu.VMEM((CHUNKS, 256, CW), BF16),
            pltpu.VMEM((CHUNKS, PLANE, ROWS, CW), BF16),
            pltpu.VMEM((CHUNKS, PLANE, ROWS, CW), BF16),
            pltpu.VMEM((CHUNKS, NZ, ROWS, CW), F32),
            pltpu.VMEM((CHUNKS, NZ, ROWS, CW), BF16),
            pltpu.VMEM((CHUNKS, NZ + 1, ROWS, CW), BF16),
            dma((3,)),
            dma((NZ,)), dma((NZ,)),
            dma((CHUNKS, NZ)), dma((CHUNKS, NZ)),
            dma((CHUNKS,)), dma((CHUNKS,)),
            dma((CHUNKS,)), dma((CHUNKS,)),
            dma((CHUNKS,)), dma((CHUNKS,)),
            dma((CHUNKS,)), dma((CHUNKS,)),
            dma((CHUNKS, NZ)), dma((CHUNKS, NZ + 1)),
        ],
        compiler_params=pltpu.CompilerParams(
            collective_id=0, has_side_effects=True, vmem_limit_bytes=60 * 2**20
        ),
        name="moe",
    )(
        tokens, routes, route_gates, placement.reshape(1, -1), swap_flags.reshape(1, -1),
        gate_weight, up_weight, down_weight,
    )


def solution(mesh):
    return jax.shard_map(
        on_device,
        mesh=mesh,
        in_specs=(
            P(("dp", "expert"), None),
            P(("dp", "expert"), None),
            P(("dp", "expert"), None),
            P(),
            P(),
            P("expert", None, "dp"),
            P("expert", None, "dp"),
            P("expert", "dp", None),
        ),
        out_specs=P(("dp", "expert"), None),
        check_vma=False,
    )
```

```python
import jax
import jax.numpy as jnp
from jax import lax
from jax.experimental import pallas as pl
from jax.experimental.pallas import tpu as pltpu
from jax.sharding import PartitionSpec as P

NX, NY, NZ = 4, 4, 8
OFFSETS = (
    (0, 0), (1, 0), (3, 0), (0, 1), (0, 3), (2, 0), (0, 2), (2, 2),
    (1, 1), (3, 3), (1, 3), (3, 1), (1, 2), (3, 2), (2, 1), (2, 3),
)
PLANE = len(OFFSETS)
GROUPS = 2
PEERS = PLANE // GROUPS
ROWS = 16
WIDE = 4096
HALF = 384
TILE = 256
GO_WIDTHS = (512, 1024, 1024, 1024, 512)
BACK_WIDTHS = (512, 1024, 1024, 1024, 512)
MESH = pl.DeviceIdType.MESH
F32 = jnp.float32
BF16 = jnp.bfloat16


def spans(widths):
    starts = [sum(widths[:c]) for c in range(len(widths))]
    return list(zip(starts, widths))


GO = spans(GO_WIDTHS)
BACK = spans(BACK_WIDTHS)


def dot(a, b):
    return jnp.dot(a, b, preferred_element_type=F32)


def kernel(
    tokens, routes, gates, placement, flags, w_gate, w_up, w_down, out,
    tok, turned, meta, sel, comb, comb_t, away, rows, w_in, w_out, acc, hid,
    mine, theirs, got, ret, back, part, hop_out, hop_in,
    w_sem, meta_send, meta_recv, ag_send, ag_recv, go_send, go_recv, sib_send, sib_recv,
    half_send, half_recv, back_send, back_recv, rs_send, rs_recv,
):
    dp = lax.axis_index("dp")
    ex = lax.axis_index("expert")
    x, core = dp // 2, dp % 2
    y, z = ex // NZ, ex % NZ
    sibling = (x * 2 + (1 - core), ex)

    def along_z(by):
        return (dp, y * NZ + (z + by + NZ) % NZ)

    def in_plane(d, sign):
        dx, dy = OFFSETS[d]
        return (((x + sign * dx + NX) % NX) * 2 + core, ((y + sign * dy + NY) % NY) * NZ + z)

    def remote(src, dst, send, recv, device):
        return pltpu.make_async_remote_copy(
            src_ref=src, dst_ref=dst, send_sem=send, recv_sem=recv, device_id=device, device_id_type=MESH
        )

    barrier = pltpu.get_barrier_semaphore()
    for i in range(1, NZ):
        pl.semaphore_signal(barrier, inc=1, device_id=along_z(i), device_id_type=MESH)
    for d in range(1, PLANE):
        pl.semaphore_signal(barrier, inc=1, device_id=in_plane(d, 1), device_id_type=MESH)
    pl.semaphore_signal(barrier, inc=1, device_id=sibling, device_id_type=MESH)

    loads = (
        pltpu.make_async_copy(w_gate.at[0], w_in.at[:, pl.ds(0, HALF)], w_sem.at[0]),
        pltpu.make_async_copy(w_up.at[0], w_in.at[:, pl.ds(HALF, HALF)], w_sem.at[1]),
        pltpu.make_async_copy(w_down.at[0], w_out, w_sem.at[2]),
    )
    for load in loads:
        load.start()

    tok[0] = tokens[...]
    turned[...] = jnp.zeros((128, 128), F32)
    turned[0:8, 0:ROWS] = routes[...].astype(F32)
    turned[8:16, 0:ROWS] = gates[...]
    meta[0] = turned[...].T[0:ROWS]

    lane = lax.broadcasted_iota(jnp.int32, (128, 128), 1)
    line = lax.broadcasted_iota(jnp.int32, (128, 128), 0)
    lane_f = lane.astype(F32)
    placed = jnp.broadcast_to(placement[...].astype(F32), (128, 128)).T
    flag = jnp.sum(
        jnp.where(placed == lane_f, jnp.broadcast_to(flags[...].astype(F32), (128, 128)), 0.0), axis=1, keepdims=True
    )
    holder = jnp.where(flag == 0.0, placed, jnp.where(placed >= 64.0, placed - 64.0, placed + 64.0))
    slot = lax.broadcasted_iota(jnp.int32, (8, 128), 1)
    far_x = jnp.zeros((8, 128), jnp.int32)
    far_y = jnp.zeros((8, 128), jnp.int32)
    for d, (dx, dy) in enumerate(OFFSETS):
        here = (slot & (PLANE - 1)) == d
        far_x = jnp.where(here, dx, far_x)
        far_y = jnp.where(here, dy, far_y)
    spot = (((far_y + y) & (NY - 1)) * NZ + z) * NX + ((far_x + x) & (NX - 1))
    spot = jnp.where(slot < 2 * PLANE, spot, -1).astype(F32)[0:1]
    where_to = jnp.where(holder == spot, 1.0, 0.0).astype(BF16)

    pl.semaphore_wait(barrier, NZ - 1 + PLANE - 1 + 1)

    meta_copies = [
        remote(meta.at[0], meta.at[i], meta_send.at[i], meta_recv.at[i], along_z(-i)) for i in range(1, NZ)
    ]
    gather = {}

    def ag(c, src, dst, by):
        cols = pl.ds(*GO[c])
        gather[(c, dst)] = remote(
            tok.at[src, :, cols], tok.at[dst, :, cols], ag_send.at[c, dst], ag_recv.at[c, dst], along_z(by)
        )
        gather[(c, dst)].start()

    for c in range(len(GO)):
        for i in (4, 3, 5, 2, 6, 1, 7):
            ag(c, 0, i, -i)
        if c == 0:
            for copy in meta_copies:
                copy.start()

    for copy in meta_copies:
        copy.wait_recv()
    info = meta[...].reshape(NZ * ROWS, 128)
    named = jnp.zeros((128, 128), F32)
    weight = jnp.zeros((128, 128), F32)
    for k in range(8):
        hit = info[:, k:k + 1] == lane_f
        named = named + jnp.where(hit, 1.0, 0.0)
        weight = weight + jnp.where(hit, info[:, 8 + k:9 + k], 0.0)
    at = dot(named.astype(BF16), where_to)
    before = jnp.where(((line >> 4) == (lane >> 4)) & (lane < line), 1.0, 0.0).astype(BF16)
    rank = dot(before, at.astype(BF16))
    pick = jnp.where(rank == (lane >> 4).astype(F32), at, 0.0)
    own = lax.broadcasted_iota(jnp.int32, (NZ, 128), 0) == (lax.broadcasted_iota(jnp.int32, (NZ, 128), 1) >> 4)

    def spread(table, r):
        return jnp.where(own[None], table[r * PLANE:(r + 1) * PLANE][:, None, :], 0.0)

    picked = pick.T
    for r in range(2):
        sel[:, r] = spread(picked, r)
    chosen = sel[...].reshape(256, 128).astype(BF16)

    def go(g, c, p):
        cols = pl.ds(*GO[c])
        return remote(
            away.at[g, p, :, cols], rows.at[g, 0, p, :, cols], go_send.at[g, c], go_recv.at[g, c], in_plane(g * PEERS + p, 1)
        )

    def all_but_self(g):
        return pl.ds(1, PEERS - 1) if g == 0 else pl.ds(0, PEERS)

    def go_all(g, c):
        cols = pl.ds(*GO[c])
        return remote(
            away.at[g, all_but_self(g), :, cols], rows.at[g, 0, all_but_self(g), :, cols],
            go_send.at[g, c], go_recv.at[g, c], sibling,
        )

    def go_out(g, c):
        for p in range(1 - g, PEERS):
            go(g, c, p).start()

    last_go = len(GO) - 1
    for c, (start, width) in enumerate(GO):
        for i in range(1, NZ):
            gather[(c, i)].wait_recv()
        for n in range(start, start + width, TILE):
            block = tok[:, :, n:n + TILE].reshape(NZ * ROWS, TILE)
            piece = dot(chosen, block).astype(BF16).reshape(GROUPS, PEERS, ROWS, TILE)
            away[:, :, :, n:n + TILE] = piece
            rows[0, 0, 0, :, n:n + TILE] = piece[0, 0]
        go_out(0, c)
        go_out(1, c)

    high = weight.astype(BF16)
    low = (weight - high.astype(F32)).astype(BF16)
    for t, share_of in enumerate((high, low)):
        table = (dot(share_of, where_to) * pick).T
        for r in range(2):
            comb[:, r] = spread(table, r)
        flat = comb[...].reshape(256, 128)
        for g in range(GROUPS):
            comb_t[g, t * 128:(t + 1) * 128] = flat[g * 128:(g + 1) * 128].T.astype(BF16)

    for load in loads[:2]:
        load.wait()

    def share(g, c):
        cols = pl.ds(*GO[c])
        return remote(rows.at[g, 0, :, :, cols], rows.at[g, 1, :, :, cols], sib_send.at[g, c], sib_recv.at[g, c], sibling)

    def first(g, c):
        start, width = GO[c]
        block = rows[g, :, :, :, start:start + width].reshape(2 * PEERS * ROWS, width)
        for n in range(0, 2 * HALF, TILE):
            term = dot(block, w_in[start:start + width, n:n + TILE])
            if c == 0:
                acc[g, :, n:n + TILE] = term
            else:
                acc[g, :, n:n + TILE] += term

    def pair(g, c):
        cols = pl.ds(*BACK[c])
        return remote(theirs.at[g, :, cols], got.at[g, :, cols], half_send.at[g, c], half_recv.at[g, c], sibling)

    def home(g, c, p):
        cols = pl.ds(*BACK[c])
        return remote(
            ret.at[g, p, :, cols], back.at[g, p, :, cols], back_send.at[g, c], back_recv.at[g, c], in_plane(g * PEERS + p, -1)
        )

    def home_all(g, c):
        cols = pl.ds(*BACK[c])
        return remote(
            ret.at[g, all_but_self(g), :, cols], back.at[g, all_but_self(g), :, cols],
            back_send.at[g, c], back_recv.at[g, c], sibling,
        )

    def finish(g, c):
        start, width = BACK[c]
        cols = slice(start, start + width)
        pair(g, c).wait_recv()
        both = (mine[g, :, cols].astype(F32) + got[g, :, cols].astype(F32)).astype(BF16).reshape(PEERS, ROWS, width)
        ret[g, :, :, cols] = both
        if g == 0:
            back[0, 0, :, cols] = both[0]
        for p in range(1 - g, PEERS):
            home(g, c, p).start()

    def arrived(g, c):
        go_all(g, c).wait_recv()
        share(g, c).start()
        if c > 0:
            share(g, c - 1).wait_recv()
            first(g, c - 1)
        if c == last_go:
            share(g, c).wait_recv()
            first(g, c)

    def activate(g):
        gate_act = acc[g, :, 0:HALF]
        hid[g] = (gate_act / (1.0 + jnp.exp(-gate_act)) * acc[g, :, HALF:2 * HALF]).astype(BF16)

    def second(g, c):
        start, width = BACK[c]
        for n in range(start, start + width, TILE):
            two = dot(hid[g], w_out[:, n:n + TILE]).astype(BF16)
            mine[g, :, n:n + TILE] = two[0:128]
            theirs[g, :, n:n + TILE] = two[128:256]
        pair(g, c).start()

    for c in range(len(GO)):
        arrived(0, c)
    activate(0)
    loads[2].wait()
    for c in range(len(BACK)):
        second(0, c)
        if c > 0:
            finish(0, c - 1)
    finish(0, len(BACK) - 1)
    for c in range(len(GO)):
        arrived(1, c)
    activate(1)
    for c in range(len(BACK)):
        second(1, c)
        if c > 0:
            finish(1, c - 1)
    finish(1, len(BACK) - 1)

    def gathered(g, c):
        start, width = BACK[c]
        home_all(g, c).wait_recv()
        for n in range(start, start + width, TILE):
            block = back[g, :, :, n:n + TILE].reshape(PEERS * ROWS, TILE)
            two = dot(comb_t[g], block)
            two = (two[0:128] + two[128:256]).reshape(NZ, ROWS, TILE)
            if g == 0:
                part[:, :, n:n + TILE] = two
            else:
                part[:, :, n:n + TILE] += two

    def rs(c, src, dst, by):
        cols = pl.ds(*BACK[c])
        return remote(
            hop_out.at[src, :, cols], hop_in.at[dst, :, cols], rs_send.at[c, src], rs_recv.at[c, dst], along_z(by)
        )

    last = len(BACK) - 1

    def rs_to_mid(c):
        if c == last:
            return ()
        return (rs(c, 3, 4, 1), rs(c, 5, 5, -1), rs(c, 4, 6, 2 if c % 2 == 0 else -2))

    def rs_near(c):
        if c == last:
            return tuple(rs(c, i, i - 1, i) for i in (4, 3, 5, 2, 6, 1, 7))
        return (rs(c, 1, 0, 1), rs(c, 7, 1, -1))

    def rs_second(c):
        if c == last:
            return ()
        return (rs(c, 2, 2, 2), rs(c, 6, 3, -2))

    def middle(c):
        start, width = BACK[c]
        cols = slice(start, start + width)
        for copy in rs_to_mid(c):
            copy.wait_recv()
        up = part[2, :, cols] + hop_in[4, :, cols].astype(F32)
        down = part[6, :, cols] + hop_in[5, :, cols].astype(F32)
        if c % 2 == 0:
            up = up + hop_in[6, :, cols].astype(F32)
        else:
            down = down + hop_in[6, :, cols].astype(F32)
        hop_out[2, :, cols] = up.astype(BF16)
        hop_out[6, :, cols] = down.astype(BF16)
        for copy in rs_second(c):
            copy.start()

    def done(c):
        start, width = BACK[c]
        cols = slice(start, start + width)
        for copy in rs_near(c) + rs_second(c):
            copy.wait_recv()
        total = part[0, :, cols]
        for i in range(NZ - 1 if c == last else 4):
            total = total + hop_in[i, :, cols].astype(F32)
        out[:, cols] = total.astype(BF16)

    for c in range(len(BACK)):
        gathered(0, c)

    for c in range(last + 1):
        start, width = BACK[c]
        cols = slice(start, start + width)
        gathered(1, c)
        for i in (4, 3, 5, 2, 6, 1, 7) if c == last else (4, 3, 5, 1, 7):
            hop_out[i, :, cols] = part[i, :, cols].astype(BF16)
        for copy in rs_to_mid(c) + rs_near(c):
            copy.start()
        if c > 0:
            middle(c - 1)
        if c > 1:
            done(c - 2)
    done(last - 1)
    done(last)

    for copy in meta_copies:
        copy.wait_send()
    for copy in gather.values():
        copy.wait_send()
    for g in range(GROUPS):
        for c in range(len(GO)):
            go_all(g, c).wait_send()
            share(g, c).wait_send()
        for c in range(len(BACK)):
            pair(g, c).wait_send()
            home_all(g, c).wait_send()
    for c in range(len(BACK)):
        for copy in rs_to_mid(c) + rs_near(c) + rs_second(c):
            copy.wait_send()


def on_device(tokens, routes, route_gates, placement, swap_flags, gate_weight, up_weight, down_weight):
    vmem = pl.BlockSpec(memory_space=pltpu.VMEM)
    hbm = pl.BlockSpec(memory_space=pl.ANY)
    dma = pltpu.SemaphoreType.DMA
    lanes = PEERS * ROWS
    n_go, n_back = len(GO), len(BACK)
    return pl.pallas_call(
        kernel,
        out_shape=jax.ShapeDtypeStruct(tokens.shape, tokens.dtype),
        in_specs=[vmem] * 5 + [hbm] * 3,
        out_specs=vmem,
        scratch_shapes=[
            pltpu.VMEM((NZ, ROWS, WIDE), BF16),
            pltpu.VMEM((128, 128), F32),
            pltpu.VMEM((NZ, ROWS, 128), F32),
            pltpu.VMEM((PLANE, 2, NZ, 128), F32),
            pltpu.VMEM((PLANE, 2, NZ, 128), F32),
            pltpu.VMEM((GROUPS, 256, lanes), BF16),
            pltpu.VMEM((GROUPS, PEERS, ROWS, WIDE), BF16),
            pltpu.VMEM((GROUPS, 2, PEERS, ROWS, WIDE), BF16),
            pltpu.VMEM((WIDE, 2 * HALF), BF16),
            pltpu.VMEM((HALF, WIDE), BF16),
            pltpu.VMEM((GROUPS, 2 * lanes, 2 * HALF), F32),
            pltpu.VMEM((GROUPS, 2 * lanes, HALF), BF16),
            pltpu.VMEM((GROUPS, lanes, WIDE), BF16),
            pltpu.VMEM((GROUPS, lanes, WIDE), BF16),
            pltpu.VMEM((GROUPS, lanes, WIDE), BF16),
            pltpu.VMEM((GROUPS, PEERS, ROWS, WIDE), BF16),
            pltpu.VMEM((GROUPS, PEERS, ROWS, WIDE), BF16),
            pltpu.VMEM((NZ, ROWS, WIDE), F32),
            pltpu.VMEM((NZ, ROWS, WIDE), BF16),
            pltpu.VMEM((NZ - 1, ROWS, WIDE), BF16),
            dma((3,)),
            dma((NZ,)), dma((NZ,)),
            dma((n_go, NZ)), dma((n_go, NZ)),
            dma((GROUPS, n_go)), dma((GROUPS, n_go)),
            dma((GROUPS, n_go)), dma((GROUPS, n_go)),
            dma((GROUPS, n_back)), dma((GROUPS, n_back)),
            dma((GROUPS, n_back)), dma((GROUPS, n_back)),
            dma((n_back, NZ)), dma((n_back, NZ - 1)),
        ],
        compiler_params=pltpu.CompilerParams(
            collective_id=0, has_side_effects=True, vmem_limit_bytes=60 * 2**20
        ),
        name="moe",
    )(
        tokens, routes.T, route_gates.T, placement.reshape(1, -1), swap_flags.reshape(1, -1),
        gate_weight, up_weight, down_weight,
    )


def solution(mesh):
    return jax.shard_map(
        on_device,
        mesh=mesh,
        in_specs=(
            P(("dp", "expert"), None),
            P(("dp", "expert"), None),
            P(("dp", "expert"), None),
            P(),
            P(),
            P("expert", None, "dp"),
            P("expert", None, "dp"),
            P("expert", "dp", None),
        ),
        out_specs=P(("dp", "expert"), None),
        check_vma=False,
    )
```

```python
import jax
import jax.numpy as jnp
from jax import lax
from jax.experimental import pallas as pl
from jax.experimental.pallas import tpu as pltpu
from jax.sharding import PartitionSpec as P

NX, NY, NZ = 4, 4, 8
OFFSETS = (
    (0, 0), (1, 0), (3, 0), (0, 1), (0, 3), (2, 0), (0, 2), (2, 2),
    (1, 1), (3, 3), (1, 3), (3, 1), (1, 2), (3, 2), (2, 1), (2, 3),
)
PLANE = len(OFFSETS)
SOURCES = (0, 1, 2, 7, 3, 4, 5, 6)
GROUPS = 2
NEAR = NZ // GROUPS
ROWS = 16
SOME = 2 * NEAR
WIDE = 4096
HALF = 384
TILE = 256
GO_WIDTHS = ((512, 1536, 2048), (1024, 1024, 1024, 1024))
BACK_WIDTHS = ((1024, 3072), (1024, 1024, 1024, 512, 512))
MESH = pl.DeviceIdType.MESH
F32 = jnp.float32
BF16 = jnp.bfloat16


def spans(widths):
    starts = [sum(widths[:c]) for c in range(len(widths))]
    return list(zip(starts, widths))


GO = tuple(spans(widths) for widths in GO_WIDTHS)
BACK = tuple(spans(widths) for widths in BACK_WIDTHS)
MOST_GO = max(len(widths) for widths in GO)
MOST_BACK = max(len(widths) for widths in BACK)


def dot(a, b):
    return jnp.dot(a, b, preferred_element_type=F32)


def kernel(
    tokens, routes, gates, placement, flags, w_gate, w_up, w_down, out,
    tok, turned, meta, sel, comb_t, away, rows, w_in, w_out, acc, hid,
    mine, theirs, got, ret, back, part, hop_out, hop_in,
    w_sem, meta_send, meta_recv, ag_send, ag_recv, go_send, go_recv, sib_send, sib_recv,
    half_send, half_recv, back_send, back_recv, rs_send, rs_recv,
):
    dp = lax.axis_index("dp")
    ex = lax.axis_index("expert")
    x, core = dp // 2, dp % 2
    y, z = ex // NZ, ex % NZ
    sibling = (x * 2 + (1 - core), ex)

    def along_z(by):
        return (dp, y * NZ + (z + by * (1 - 2 * core) + NZ) % NZ)

    def in_plane(d, sign):
        dx, dy = OFFSETS[d]
        return (((x + sign * dx + NX) % NX) * 2 + core, ((y + sign * dy + NY) % NY) * NZ + z)

    def remote(src, dst, send, recv, device):
        return pltpu.make_async_remote_copy(
            src_ref=src, dst_ref=dst, send_sem=send, recv_sem=recv, device_id=device, device_id_type=MESH
        )

    barrier = pltpu.get_barrier_semaphore()
    for i in range(1, NZ):
        pl.semaphore_signal(barrier, inc=1, device_id=along_z(i), device_id_type=MESH)
    for d in range(1, PLANE):
        pl.semaphore_signal(barrier, inc=1, device_id=in_plane(d, 1), device_id_type=MESH)
    pl.semaphore_signal(barrier, inc=1, device_id=sibling, device_id_type=MESH)

    loads = (
        pltpu.make_async_copy(w_gate.at[0], w_in.at[:, pl.ds(0, HALF)], w_sem.at[0]),
        pltpu.make_async_copy(w_up.at[0], w_in.at[:, pl.ds(HALF, HALF)], w_sem.at[1]),
        pltpu.make_async_copy(w_down.at[0], w_out, w_sem.at[2]),
    )
    for load in loads:
        load.start()

    tok[0] = tokens[...]
    turned[...] = jnp.zeros((128, 128), F32)
    turned[0:8, 0:ROWS] = routes[...].astype(F32)
    turned[8:16, 0:ROWS] = gates[...]
    meta[0] = turned[...].T[0:ROWS]

    lane = lax.broadcasted_iota(jnp.int32, (128, 128), 1)
    line = lax.broadcasted_iota(jnp.int32, (128, 128), 0)
    lane_f = lane.astype(F32)
    placed = jnp.broadcast_to(placement[...].astype(F32), (128, 128)).T
    flag = jnp.sum(
        jnp.where(placed == lane_f, jnp.broadcast_to(flags[...].astype(F32), (128, 128)), 0.0), axis=1, keepdims=True
    )
    holder = jnp.where(flag == 0.0, placed, jnp.where(placed >= 64.0, placed - 64.0, placed + 64.0))
    slot = lax.broadcasted_iota(jnp.int32, (8, 128), 1)
    far_x = jnp.zeros((8, 128), jnp.int32)
    far_y = jnp.zeros((8, 128), jnp.int32)
    for d, (dx, dy) in enumerate(OFFSETS):
        here = (slot & (PLANE - 1)) == d
        far_x = jnp.where(here, dx, far_x)
        far_y = jnp.where(here, dy, far_y)
    spot = (((far_y + y) & (NY - 1)) * NZ + z) * NX + ((far_x + x) & (NX - 1))
    spot = jnp.where(slot < 2 * PLANE, spot, -1).astype(F32)[0:1]
    where_to = jnp.where(holder == spot, 1.0, 0.0).astype(BF16)

    pl.semaphore_wait(barrier, NZ - 1 + PLANE - 1 + 1)

    meta_copies = [
        remote(meta.at[0], meta.at[q], meta_send.at[q], meta_recv.at[q], along_z(-SOURCES[q])) for q in range(1, NZ)
    ]
    gather = {}

    def ag(g, c, q):
        cols = pl.ds(*GO[g][c])
        gather[(g, c, q)] = remote(
            tok.at[0, :, cols], tok.at[q, :, cols], ag_send.at[c, q], ag_recv.at[c, q], along_z(-SOURCES[q])
        )
        gather[(g, c, q)].start()

    def slots(g):
        return (2, 1, 3) if g == 0 else (5, 4, 6, 7)

    for g in range(GROUPS):
        for c in range(len(GO[g])):
            for q in slots(g):
                ag(g, c, q)
            if g == 0 and c == 0:
                for copy in meta_copies:
                    copy.start()

    for copy in meta_copies:
        copy.wait_recv()
    info = meta[...].reshape(NZ * ROWS, 128)
    named = jnp.zeros((128, 128), F32)
    weight = jnp.zeros((128, 128), F32)
    for k in range(8):
        hit = info[:, k:k + 1] == lane_f
        named = named + jnp.where(hit, 1.0, 0.0)
        weight = weight + jnp.where(hit, info[:, 8 + k:9 + k], 0.0)
    at = dot(named.astype(BF16), where_to)
    before = jnp.where(((line >> 4) == (lane >> 4)) & (lane < line), 1.0, 0.0).astype(BF16)
    rank = dot(before, at.astype(BF16))
    pick = jnp.where(rank == (lane >> 4).astype(F32), at, 0.0)
    spot_row = lax.broadcasted_iota(jnp.int32, (SOME, 128), 0)
    spot_slot = lax.broadcasted_iota(jnp.int32, (SOME, 128), 1) >> 4
    second_rank = spot_row >= NEAR

    def spread(table, g):
        ours = spot_slot == (spot_row & (NEAR - 1)) + g * NEAR
        both = jnp.where(second_rank[None], table[PLANE:2 * PLANE][:, None, :], table[0:PLANE][:, None, :])
        sel[...] = jnp.where(ours[None], both, 0.0)
        return sel[...].reshape(PLANE * SOME, 128).T[g * 64:(g + 1) * 64]

    picked = pick.T
    chosen = [spread(picked, g).T.astype(BF16) for g in range(GROUPS)]

    def go(g, c, p):
        cols = pl.ds(*GO[g][c])
        return remote(
            away.at[g, p, :, cols], rows.at[g, 0, p, :, cols], go_send.at[g, c], go_recv.at[g, c], in_plane(p, 1)
        )

    others = pl.ds(1, PLANE - 1)

    def go_all(g, c):
        cols = pl.ds(*GO[g][c])
        return remote(
            away.at[g, others, :, cols], rows.at[g, 0, others, :, cols], go_send.at[g, c], go_recv.at[g, c], sibling
        )

    def dispatch(g, c):
        start, width = GO[g][c]
        for q in slots(g):
            gather[(g, c, q)].wait_recv()
        for n in range(start, start + width, TILE):
            block = tok[g * NEAR:(g + 1) * NEAR, :, n:n + TILE].reshape(NEAR * ROWS, TILE)
            piece = dot(chosen[g], block).astype(BF16).reshape(PLANE, SOME, TILE)
            away[g, :, :, n:n + TILE] = piece
            rows[g, 0, 0, :, n:n + TILE] = piece[0]
        for p in range(1, PLANE):
            go(g, c, p).start()

    for c in range(len(GO[0])):
        dispatch(0, c)
    dispatch(1, 0)

    high = weight.astype(BF16)
    low = (weight - high.astype(F32)).astype(BF16)
    for t, share_of in enumerate((high, low)):
        table = (dot(share_of, where_to) * pick).T
        for g in range(GROUPS):
            comb_t[g, t * 64:(t + 1) * 64] = spread(table, g).astype(BF16)

    dispatch(1, 1)
    for load in loads:
        load.wait()

    def share(g, c):
        cols = pl.ds(*GO[g][c])
        return remote(rows.at[g, 0, :, :, cols], rows.at[g, 1, :, :, cols], sib_send.at[g, c], sib_recv.at[g, c], sibling)

    def first(g, c):
        start, width = GO[g][c]
        block = rows[g, :, :, :, start:start + width].reshape(2 * PLANE * SOME, width)
        for n in range(0, 2 * HALF, TILE):
            term = dot(block, w_in[start:start + width, n:n + TILE])
            if c == 0:
                acc[g, :, n:n + TILE] = term
            else:
                acc[g, :, n:n + TILE] += term

    def pair(g, c):
        cols = pl.ds(*BACK[g][c])
        return remote(theirs.at[g, :, cols], got.at[g, :, cols], half_send.at[g, c], half_recv.at[g, c], sibling)

    def home(g, c, p):
        cols = pl.ds(*BACK[g][c])
        return remote(
            ret.at[g, p, :, cols], back.at[g, p, :, cols], back_send.at[g, c], back_recv.at[g, c], in_plane(p, -1)
        )

    def home_all(g, c):
        cols = pl.ds(*BACK[g][c])
        return remote(
            ret.at[g, others, :, cols], back.at[g, others, :, cols], back_send.at[g, c], back_recv.at[g, c], sibling
        )

    def finish(g, c):
        start, width = BACK[g][c]
        cols = slice(start, start + width)
        pair(g, c).wait_recv()
        both = (mine[g, :, cols].astype(F32) + got[g, :, cols].astype(F32)).astype(BF16).reshape(PLANE, SOME, width)
        ret[g, :, :, cols] = both
        back[g, 0, :, cols] = both[0]
        for p in range(1, PLANE):
            home(g, c, p).start()

    def arrived(g, c):
        go_all(g, c).wait_recv()
        share(g, c).start()
        if c > 0:
            share(g, c - 1).wait_recv()
            first(g, c - 1)
        if c == len(GO[g]) - 1:
            share(g, c).wait_recv()
            first(g, c)

    def activate(g):
        gate_act = acc[g, :, 0:HALF]
        hid[g] = (gate_act / (1.0 + jnp.exp(-gate_act)) * acc[g, :, HALF:2 * HALF]).astype(BF16)

    def second(g, c):
        start, width = BACK[g][c]
        for n in range(start, start + width, TILE):
            two = dot(hid[g], w_out[:, n:n + TILE]).astype(BF16)
            mine[g, :, n:n + TILE] = two[0:128]
            theirs[g, :, n:n + TILE] = two[128:256]
        pair(g, c).start()

    def experts(g):
        activate(g)
        for c in range(len(BACK[g])):
            second(g, c)
            if c > 0:
                finish(g, c - 1)
        finish(g, len(BACK[g]) - 1)

    arrived(0, 0)
    dispatch(1, 2)
    arrived(0, 1)
    arrived(0, 2)
    dispatch(1, 3)
    experts(0)
    for c in range(len(GO[1])):
        arrived(1, c)
    experts(1)

    def gathered(g, c):
        start, width = BACK[g][c]
        home_all(g, c).wait_recv()
        for n in range(start, start + width, TILE):
            block = back[g, :, :, n:n + TILE].reshape(PLANE * SOME, TILE)
            two = dot(comb_t[g], block)
            part[g * NEAR:(g + 1) * NEAR, :, n:n + TILE] = (two[0:64] + two[64:128]).reshape(NEAR, ROWS, TILE)

    ends = BACK[1]
    last = len(ends) - 1
    slot_of = {far: q for q, far in enumerate(SOURCES)}

    def rs(c, far, dst, by):
        cols = pl.ds(*ends[c])
        return remote(
            hop_out.at[far, :, cols], hop_in.at[dst, :, cols], rs_send.at[c, far], rs_recv.at[c, dst], along_z(by)
        )

    def rs_near(c):
        return rs(c, 1, 0, 1), rs(c, 7, 1, -1)

    def rs_far(c):
        if c == last:
            return tuple(rs(c, far, dst, far) for far, dst in ((4, 4), (3, 5), (5, 6), (6, 3), (2, 2)))
        return rs(c, 3, 4, 1), rs(c, 5, 5, -1), rs(c, 4, 6, 2)

    def rs_second(c):
        return () if c == last else (rs(c, 2, 2, 2), rs(c, 6, 3, -2))

    def leave(c, fars):
        start, width = ends[c]
        cols = slice(start, start + width)
        for far in fars:
            hop_out[far, :, cols] = part[slot_of[far], :, cols].astype(BF16)

    def middle(c):
        start, width = ends[c]
        cols = slice(start, start + width)
        for copy in rs_far(c):
            copy.wait_recv()
        up = part[slot_of[2], :, cols] + hop_in[4, :, cols].astype(F32) + hop_in[6, :, cols].astype(F32)
        down = part[slot_of[6], :, cols] + hop_in[5, :, cols].astype(F32)
        hop_out[2, :, cols] = up.astype(BF16)
        hop_out[6, :, cols] = down.astype(BF16)
        for copy in rs_second(c):
            copy.start()

    def done(c):
        start, width = ends[c]
        cols = slice(start, start + width)
        for copy in rs_near(c) + (rs_far(c) if c == last else rs_second(c)):
            copy.wait_recv()
        total = part[0, :, cols]
        for i in range(NZ - 1 if c == last else 4):
            total = total + hop_in[i, :, cols].astype(F32)
        out[:, cols] = total.astype(BF16)

    for c in range(len(BACK[0])):
        gathered(0, c)
    for c in range(last + 1):
        leave(c, (1, 7))
        for copy in rs_near(c):
            copy.start()
    for c in range(last + 1):
        gathered(1, c)
        leave(c, (4, 3, 5, 6, 2) if c == last else (3, 5, 4))
        for copy in rs_far(c):
            copy.start()
        if c > 0:
            middle(c - 1)
        if c > 1:
            done(c - 2)
    done(last - 1)
    done(last)

    for copy in meta_copies:
        copy.wait_send()
    for copy in gather.values():
        copy.wait_send()
    for g in range(GROUPS):
        for c in range(len(GO[g])):
            go_all(g, c).wait_send()
            share(g, c).wait_send()
        for c in range(len(BACK[g])):
            pair(g, c).wait_send()
            home_all(g, c).wait_send()
    for c in range(last + 1):
        for copy in rs_near(c) + rs_far(c) + rs_second(c):
            copy.wait_send()


def on_device(tokens, routes, route_gates, placement, swap_flags, gate_weight, up_weight, down_weight):
    vmem = pl.BlockSpec(memory_space=pltpu.VMEM)
    hbm = pl.BlockSpec(memory_space=pl.ANY)
    dma = pltpu.SemaphoreType.DMA
    lanes = PLANE * SOME
    return pl.pallas_call(
        kernel,
        out_shape=jax.ShapeDtypeStruct(tokens.shape, tokens.dtype),
        in_specs=[vmem] * 5 + [hbm] * 3,
        out_specs=vmem,
        scratch_shapes=[
            pltpu.VMEM((NZ, ROWS, WIDE), BF16),
            pltpu.VMEM((128, 128), F32),
            pltpu.VMEM((NZ, ROWS, 128), F32),
            pltpu.VMEM((PLANE, SOME, 128), F32),
            pltpu.VMEM((GROUPS, 128, lanes), BF16),
            pltpu.VMEM((GROUPS, PLANE, SOME, WIDE), BF16),
            pltpu.VMEM((GROUPS, 2, PLANE, SOME, WIDE), BF16),
            pltpu.VMEM((WIDE, 2 * HALF), BF16),
            pltpu.VMEM((HALF, WIDE), BF16),
            pltpu.VMEM((GROUPS, 2 * lanes, 2 * HALF), F32),
            pltpu.VMEM((GROUPS, 2 * lanes, HALF), BF16),
            pltpu.VMEM((GROUPS, lanes, WIDE), BF16),
            pltpu.VMEM((GROUPS, lanes, WIDE), BF16),
            pltpu.VMEM((GROUPS, lanes, WIDE), BF16),
            pltpu.VMEM((GROUPS, PLANE, SOME, WIDE), BF16),
            pltpu.VMEM((GROUPS, PLANE, SOME, WIDE), BF16),
            pltpu.VMEM((NZ, ROWS, WIDE), F32),
            pltpu.VMEM((NZ, ROWS, WIDE), BF16),
            pltpu.VMEM((NZ - 1, ROWS, WIDE), BF16),
            dma((3,)),
            dma((NZ,)), dma((NZ,)),
            dma((MOST_GO, NZ)), dma((MOST_GO, NZ)),
            dma((GROUPS, MOST_GO)), dma((GROUPS, MOST_GO)),
            dma((GROUPS, MOST_GO)), dma((GROUPS, MOST_GO)),
            dma((GROUPS, MOST_BACK)), dma((GROUPS, MOST_BACK)),
            dma((GROUPS, MOST_BACK)), dma((GROUPS, MOST_BACK)),
            dma((MOST_BACK, NZ)), dma((MOST_BACK, NZ - 1)),
        ],
        compiler_params=pltpu.CompilerParams(
            collective_id=0, has_side_effects=True, vmem_limit_bytes=60 * 2**20
        ),
        name="moe",
    )(
        tokens, routes.T, route_gates.T, placement.reshape(1, -1), swap_flags.reshape(1, -1),
        gate_weight, up_weight, down_weight,
    )


def solution(mesh):
    return jax.shard_map(
        on_device,
        mesh=mesh,
        in_specs=(
            P(("dp", "expert"), None),
            P(("dp", "expert"), None),
            P(("dp", "expert"), None),
            P(),
            P(),
            P("expert", None, "dp"),
            P("expert", None, "dp"),
            P("expert", "dp", None),
        ),
        out_specs=P(("dp", "expert"), None),
        check_vma=False,
    )
```

```python
import jax
import jax.numpy as jnp
from jax import lax
from jax.experimental import pallas as pl
from jax.experimental.pallas import tpu as pltpu
from jax.sharding import PartitionSpec as P

NX, NY, NZ = 4, 4, 8
OFFSETS = (
    (0, 0), (1, 0), (3, 0), (0, 1), (0, 3), (2, 0), (0, 2), (2, 2),
    (1, 1), (3, 3), (1, 3), (3, 1), (1, 2), (3, 2), (2, 1), (2, 3),
)
PLANE = len(OFFSETS)
SOURCES = (0, 1, 2, 7, 3, 4, 5, 6)
GROUPS = 2
NEAR = NZ // GROUPS
ROWS = 16
SOME = 2 * NEAR
WIDE = 4096
HALF = 384
TILE = 256
GO_WIDTHS = ((512, 1536, 2048), (1024, 1024, 1024, 1024))
BACK_WIDTHS = ((1024, 3072), (1024, 1024, 1024, 512, 512))
MESH = pl.DeviceIdType.MESH
F32 = jnp.float32
BF16 = jnp.bfloat16


def spans(widths):
    starts = [sum(widths[:c]) for c in range(len(widths))]
    return list(zip(starts, widths))


GO = tuple(spans(widths) for widths in GO_WIDTHS)
BACK = tuple(spans(widths) for widths in BACK_WIDTHS)
MOST_GO = max(len(widths) for widths in GO)
MOST_BACK = max(len(widths) for widths in BACK)


def dot(a, b):
    return jnp.dot(a, b, preferred_element_type=F32)


def kernel(
    tokens, routes_in, gates_in, placement_in, flags_in, w_gate, w_up, w_down, out,
    routes, gates, placement, flags, summed, in_sem, out_sem,
    tok, turned, meta, sel, comb_t, away, rows, w_in, w_out, acc, hid,
    mine, theirs, got, ret, back, part, hop_out, hop_in,
    w_sem, meta_send, meta_recv, ag_send, ag_recv, go_send, go_recv, sib_send, sib_recv,
    half_send, half_recv, back_send, back_recv, rs_send, rs_recv,
):
    dp = lax.axis_index("dp")
    ex = lax.axis_index("expert")
    x, core = dp // 2, dp % 2
    y, z = ex // NZ, ex % NZ
    sibling = (x * 2 + (1 - core), ex)

    def along_z(by):
        return (dp, y * NZ + (z + by * (1 - 2 * core) + NZ) % NZ)

    def in_plane(d, sign):
        dx, dy = OFFSETS[d]
        return (((x + sign * dx + NX) % NX) * 2 + core, ((y + sign * dy + NY) % NY) * NZ + z)

    def remote(src, dst, send, recv, device):
        return pltpu.make_async_remote_copy(
            src_ref=src, dst_ref=dst, send_sem=send, recv_sem=recv, device_id=device, device_id_type=MESH
        )

    barrier = pltpu.get_barrier_semaphore()
    for i in range(1, NZ):
        pl.semaphore_signal(barrier, inc=1, device_id=along_z(i), device_id_type=MESH)
    for d in range(1, PLANE):
        pl.semaphore_signal(barrier, inc=1, device_id=in_plane(d, 1), device_id_type=MESH)
    pl.semaphore_signal(barrier, inc=1, device_id=sibling, device_id_type=MESH)

    loads = (
        pltpu.make_async_copy(w_gate.at[0], w_in.at[:, pl.ds(0, HALF)], w_sem.at[0]),
        pltpu.make_async_copy(w_up.at[0], w_in.at[:, pl.ds(HALF, HALF)], w_sem.at[1]),
        pltpu.make_async_copy(w_down.at[0], w_out, w_sem.at[2]),
    )
    small = (
        pltpu.make_async_copy(routes_in, routes, in_sem.at[0]),
        pltpu.make_async_copy(gates_in, gates, in_sem.at[1]),
        pltpu.make_async_copy(placement_in, placement, in_sem.at[2]),
        pltpu.make_async_copy(flags_in, flags, in_sem.at[3]),
        pltpu.make_async_copy(tokens, tok.at[0], in_sem.at[4]),
    )
    for load in small + loads:
        load.start()
    for load in small:
        load.wait()

    turned[...] = jnp.zeros((128, 128), F32)
    turned[0:8, 0:ROWS] = routes[...].astype(F32)
    turned[8:16, 0:ROWS] = gates[...]
    meta[0] = turned[...].T[0:ROWS]

    pl.semaphore_wait(barrier, NZ - 1 + PLANE - 1 + 1)

    meta_copies = [
        remote(meta.at[0], meta.at[q], meta_send.at[q], meta_recv.at[q], along_z(-SOURCES[q])) for q in range(1, NZ)
    ]
    gather = {}

    def ag(g, c, q, src, by):
        cols = pl.ds(*GO[g][c])
        gather[(g, c, q)] = remote(
            src.at[:, cols], tok.at[q, :, cols], ag_send.at[c, q], ag_recv.at[c, q], along_z(by)
        )
        gather[(g, c, q)].start()

    for c in range(len(GO[0])):
        for q in (2, 1, 3):
            ag(0, c, q, tok.at[0], -SOURCES[q])
        if c == 0:
            for copy in meta_copies:
                copy.start()

    def forward(c):
        ag(1, c, 5, tok.at[2], -2)
        ag(1, c, 6, tok.at[3], 2)
        ag(1, c, 4, tok.at[2], -1)
        ag(1, c, 7, tok.at[3], 1)

    lane = lax.broadcasted_iota(jnp.int32, (128, 128), 1)
    line = lax.broadcasted_iota(jnp.int32, (128, 128), 0)
    lane_f = lane.astype(F32)
    placed = jnp.broadcast_to(placement[...].astype(F32), (128, 128)).T
    flag = jnp.sum(
        jnp.where(placed == lane_f, jnp.broadcast_to(flags[...].astype(F32), (128, 128)), 0.0), axis=1, keepdims=True
    )
    holder = jnp.where(flag == 0.0, placed, jnp.where(placed >= 64.0, placed - 64.0, placed + 64.0))
    slot = lax.broadcasted_iota(jnp.int32, (8, 128), 1)
    far_x = jnp.zeros((8, 128), jnp.int32)
    far_y = jnp.zeros((8, 128), jnp.int32)
    for d, (dx, dy) in enumerate(OFFSETS):
        here = (slot & (PLANE - 1)) == d
        far_x = jnp.where(here, dx, far_x)
        far_y = jnp.where(here, dy, far_y)
    spot = (((far_y + y) & (NY - 1)) * NZ + z) * NX + ((far_x + x) & (NX - 1))
    spot = jnp.where(slot < 2 * PLANE, spot, -1).astype(F32)[0:1]
    where_to = jnp.where(holder == spot, 1.0, 0.0).astype(BF16)

    for copy in meta_copies:
        copy.wait_recv()
    info = meta[...].reshape(NZ * ROWS, 128)
    named = jnp.zeros((128, 128), F32)
    weight = jnp.zeros((128, 128), F32)
    for k in range(8):
        hit = info[:, k:k + 1] == lane_f
        named = named + jnp.where(hit, 1.0, 0.0)
        weight = weight + jnp.where(hit, info[:, 8 + k:9 + k], 0.0)
    at = dot(named.astype(BF16), where_to)
    before = jnp.where(((line >> 4) == (lane >> 4)) & (lane < line), 1.0, 0.0).astype(BF16)
    rank = dot(before, at.astype(BF16))
    pick = jnp.where(rank == (lane >> 4).astype(F32), at, 0.0)
    spot_row = lax.broadcasted_iota(jnp.int32, (SOME, 128), 0)
    spot_slot = lax.broadcasted_iota(jnp.int32, (SOME, 128), 1) >> 4
    second_rank = spot_row >= NEAR

    def spread(table, g):
        ours = spot_slot == (spot_row & (NEAR - 1)) + g * NEAR
        both = jnp.where(second_rank[None], table[PLANE:2 * PLANE][:, None, :], table[0:PLANE][:, None, :])
        sel[...] = jnp.where(ours[None], both, 0.0)
        return sel[...].reshape(PLANE * SOME, 128).T[g * 64:(g + 1) * 64]

    picked = pick.T
    chosen = [spread(picked, g).T.astype(BF16) for g in range(GROUPS)]

    def go(g, c, p):
        cols = pl.ds(*GO[g][c])
        return remote(
            away.at[g, p, :, cols], rows.at[g, 0, p, :, cols], go_send.at[g, c], go_recv.at[g, c], in_plane(p, 1)
        )

    others = pl.ds(1, PLANE - 1)

    def go_all(g, c):
        cols = pl.ds(*GO[g][c])
        return remote(
            away.at[g, others, :, cols], rows.at[g, 0, others, :, cols], go_send.at[g, c], go_recv.at[g, c], sibling
        )

    def dispatch(g, c):
        start, width = GO[g][c]
        for q in range(max(1, g * NEAR), (g + 1) * NEAR):
            gather[(g, c, q)].wait_recv()
        if g == 0:
            for far in range(len(GO[1])):
                if start < sum(GO[1][far]) <= start + width:
                    forward(far)
        for n in range(start, start + width, TILE):
            block = tok[g * NEAR:(g + 1) * NEAR, :, n:n + TILE].reshape(NEAR * ROWS, TILE)
            piece = dot(chosen[g], block).astype(BF16).reshape(PLANE, SOME, TILE)
            away[g, :, :, n:n + TILE] = piece
            rows[g, 0, 0, :, n:n + TILE] = piece[0]
        for p in range(1, PLANE):
            go(g, c, p).start()

    for c in range(len(GO[0])):
        dispatch(0, c)
    dispatch(1, 0)

    high = weight.astype(BF16)
    low = (weight - high.astype(F32)).astype(BF16)
    for t, share_of in enumerate((high, low)):
        table = (dot(share_of, where_to) * pick).T
        for g in range(GROUPS):
            comb_t[g, t * 64:(t + 1) * 64] = spread(table, g).astype(BF16)

    dispatch(1, 1)
    for load in loads:
        load.wait()

    def share(g, c):
        cols = pl.ds(*GO[g][c])
        return remote(rows.at[g, 0, :, :, cols], rows.at[g, 1, :, :, cols], sib_send.at[g, c], sib_recv.at[g, c], sibling)

    def first(g, c):
        start, width = GO[g][c]
        block = rows[g, :, :, :, start:start + width].reshape(2 * PLANE * SOME, width)
        for n in range(0, 2 * HALF, TILE):
            term = dot(block, w_in[start:start + width, n:n + TILE])
            if c == 0:
                acc[g, :, n:n + TILE] = term
            else:
                acc[g, :, n:n + TILE] += term

    def pair(g, c):
        cols = pl.ds(*BACK[g][c])
        return remote(theirs.at[g, :, cols], got.at[g, :, cols], half_send.at[g, c], half_recv.at[g, c], sibling)

    def home(g, c, p):
        cols = pl.ds(*BACK[g][c])
        return remote(
            ret.at[g, p, :, cols], back.at[g, p, :, cols], back_send.at[g, c], back_recv.at[g, c], in_plane(p, -1)
        )

    def home_all(g, c):
        cols = pl.ds(*BACK[g][c])
        return remote(
            ret.at[g, others, :, cols], back.at[g, others, :, cols], back_send.at[g, c], back_recv.at[g, c], sibling
        )

    def finish(g, c):
        start, width = BACK[g][c]
        cols = slice(start, start + width)
        pair(g, c).wait_recv()
        both = (mine[g, :, cols].astype(F32) + got[g, :, cols].astype(F32)).astype(BF16).reshape(PLANE, SOME, width)
        ret[g, :, :, cols] = both
        back[g, 0, :, cols] = both[0]
        for p in range(1, PLANE):
            home(g, c, p).start()

    def arrived(g, c):
        go_all(g, c).wait_recv()
        share(g, c).start()
        if c > 0:
            share(g, c - 1).wait_recv()
            first(g, c - 1)
        if c == len(GO[g]) - 1:
            share(g, c).wait_recv()
            first(g, c)

    def activate(g):
        gate_act = acc[g, :, 0:HALF]
        hid[g] = (gate_act / (1.0 + jnp.exp(-gate_act)) * acc[g, :, HALF:2 * HALF]).astype(BF16)

    def second(g, c):
        start, width = BACK[g][c]
        for n in range(start, start + width, TILE):
            two = dot(hid[g], w_out[:, n:n + TILE]).astype(BF16)
            mine[g, :, n:n + TILE] = two[0:128]
            theirs[g, :, n:n + TILE] = two[128:256]
        pair(g, c).start()

    def experts(g):
        activate(g)
        for c in range(len(BACK[g])):
            second(g, c)
            if c > 0:
                finish(g, c - 1)
        finish(g, len(BACK[g]) - 1)

    arrived(0, 0)
    dispatch(1, 2)
    arrived(0, 1)
    arrived(0, 2)
    dispatch(1, 3)
    experts(0)
    for c in range(len(GO[1])):
        arrived(1, c)
    experts(1)

    def gathered(g, c):
        start, width = BACK[g][c]
        home_all(g, c).wait_recv()
        for n in range(start, start + width, TILE):
            block = back[g, :, :, n:n + TILE].reshape(PLANE * SOME, TILE)
            two = dot(comb_t[g], block)
            part[g * NEAR:(g + 1) * NEAR, :, n:n + TILE] = (two[0:64] + two[64:128]).reshape(NEAR, ROWS, TILE)

    ends = BACK[1]
    last = len(ends) - 1
    slot_of = {far: q for q, far in enumerate(SOURCES)}

    def rs(c, far, dst, by):
        cols = pl.ds(*ends[c])
        return remote(
            hop_out.at[far, :, cols], hop_in.at[dst, :, cols], rs_send.at[c, far], rs_recv.at[c, dst], along_z(by)
        )

    def rs_near(c):
        return rs(c, 1, 0, 1), rs(c, 7, 1, -1)

    def rs_far(c):
        if c == last:
            return tuple(rs(c, far, dst, far) for far, dst in ((4, 4), (3, 5), (5, 6), (6, 3), (2, 2)))
        return rs(c, 3, 4, 1), rs(c, 5, 5, -1), rs(c, 4, 6, 2)

    def rs_second(c):
        return () if c == last else (rs(c, 2, 2, 2), rs(c, 6, 3, -2))

    def leave(c, fars):
        start, width = ends[c]
        cols = slice(start, start + width)
        for far in fars:
            hop_out[far, :, cols] = part[slot_of[far], :, cols].astype(BF16)

    def middle(c):
        start, width = ends[c]
        cols = slice(start, start + width)
        for copy in rs_far(c):
            copy.wait_recv()
        up = part[slot_of[2], :, cols] + hop_in[4, :, cols].astype(F32) + hop_in[6, :, cols].astype(F32)
        down = part[slot_of[6], :, cols] + hop_in[5, :, cols].astype(F32)
        hop_out[2, :, cols] = up.astype(BF16)
        hop_out[6, :, cols] = down.astype(BF16)
        for copy in rs_second(c):
            copy.start()

    def written(c):
        cols = pl.ds(*ends[c])
        return pltpu.make_async_copy(summed.at[:, cols], out.at[:, cols], out_sem.at[c])

    def done(c):
        start, width = ends[c]
        cols = slice(start, start + width)
        for copy in rs_near(c) + (rs_far(c) if c == last else rs_second(c)):
            copy.wait_recv()
        total = part[0, :, cols]
        for i in range(NZ - 1 if c == last else 4):
            total = total + hop_in[i, :, cols].astype(F32)
        summed[:, cols] = total.astype(BF16)
        written(c).start()

    for c in range(len(BACK[0])):
        gathered(0, c)
    for c in range(last + 1):
        leave(c, (1, 7))
        for copy in rs_near(c):
            copy.start()
    for c in range(last + 1):
        gathered(1, c)
        leave(c, (4, 3, 5, 6, 2) if c == last else (3, 5, 4))
        for copy in rs_far(c):
            copy.start()
        if c > 0:
            middle(c - 1)
        if c > 1:
            done(c - 2)
    done(last - 1)
    done(last)

    for copy in meta_copies:
        copy.wait_send()
    for copy in gather.values():
        copy.wait_send()
    for g in range(GROUPS):
        for c in range(len(GO[g])):
            go_all(g, c).wait_send()
            share(g, c).wait_send()
        for c in range(len(BACK[g])):
            pair(g, c).wait_send()
            home_all(g, c).wait_send()
    for c in range(last + 1):
        for copy in rs_near(c) + rs_far(c) + rs_second(c):
            copy.wait_send()
        written(c).wait()


def on_device(tokens, routes, route_gates, placement, swap_flags, gate_weight, up_weight, down_weight):
    hbm = pl.BlockSpec(memory_space=pl.ANY)
    dma = pltpu.SemaphoreType.DMA
    lanes = PLANE * SOME
    return pl.pallas_call(
        kernel,
        out_shape=jax.ShapeDtypeStruct(tokens.shape, tokens.dtype),
        in_specs=[hbm] * 8,
        out_specs=hbm,
        scratch_shapes=[
            pltpu.VMEM(routes.shape[::-1], jnp.int32),
            pltpu.VMEM(route_gates.shape[::-1], F32),
            pltpu.VMEM((1, 128), jnp.int32),
            pltpu.VMEM((1, 128), jnp.int32),
            pltpu.VMEM(tokens.shape, BF16),
            dma((5,)),
            dma((MOST_BACK,)),
            pltpu.VMEM((NZ, ROWS, WIDE), BF16),
            pltpu.VMEM((128, 128), F32),
            pltpu.VMEM((NZ, ROWS, 128), F32),
            pltpu.VMEM((PLANE, SOME, 128), F32),
            pltpu.VMEM((GROUPS, 128, lanes), BF16),
            pltpu.VMEM((GROUPS, PLANE, SOME, WIDE), BF16),
            pltpu.VMEM((GROUPS, 2, PLANE, SOME, WIDE), BF16),
            pltpu.VMEM((WIDE, 2 * HALF), BF16),
            pltpu.VMEM((HALF, WIDE), BF16),
            pltpu.VMEM((GROUPS, 2 * lanes, 2 * HALF), F32),
            pltpu.VMEM((GROUPS, 2 * lanes, HALF), BF16),
            pltpu.VMEM((GROUPS, lanes, WIDE), BF16),
            pltpu.VMEM((GROUPS, lanes, WIDE), BF16),
            pltpu.VMEM((GROUPS, lanes, WIDE), BF16),
            pltpu.VMEM((GROUPS, PLANE, SOME, WIDE), BF16),
            pltpu.VMEM((GROUPS, PLANE, SOME, WIDE), BF16),
            pltpu.VMEM((NZ, ROWS, WIDE), F32),
            pltpu.VMEM((NZ, ROWS, WIDE), BF16),
            pltpu.VMEM((NZ - 1, ROWS, WIDE), BF16),
            dma((3,)),
            dma((NZ,)), dma((NZ,)),
            dma((MOST_GO, NZ)), dma((MOST_GO, NZ)),
            dma((GROUPS, MOST_GO)), dma((GROUPS, MOST_GO)),
            dma((GROUPS, MOST_GO)), dma((GROUPS, MOST_GO)),
            dma((GROUPS, MOST_BACK)), dma((GROUPS, MOST_BACK)),
            dma((GROUPS, MOST_BACK)), dma((GROUPS, MOST_BACK)),
            dma((MOST_BACK, NZ)), dma((MOST_BACK, NZ - 1)),
        ],
        compiler_params=pltpu.CompilerParams(
            collective_id=0, has_side_effects=True, vmem_limit_bytes=60 * 2**20
        ),
        name="moe",
    )(
        tokens, routes.T, route_gates.T, placement.reshape(1, -1), swap_flags.reshape(1, -1),
        gate_weight, up_weight, down_weight,
    )


def solution(mesh):
    return jax.shard_map(
        on_device,
        mesh=mesh,
        in_specs=(
            P(("dp", "expert"), None),
            P(("dp", "expert"), None),
            P(("dp", "expert"), None),
            P(),
            P(),
            P("expert", None, "dp"),
            P("expert", None, "dp"),
            P("expert", "dp", None),
        ),
        out_specs=P(("dp", "expert"), None),
        check_vma=False,
    )
```

```python
import jax
import jax.numpy as jnp
from jax import lax
from jax.experimental import pallas as pl
from jax.experimental.pallas import tpu as pltpu
from jax.sharding import PartitionSpec as P

NX, NY, NZ = 4, 4, 8
OFFSETS = (
    (0, 0), (1, 0), (3, 0), (0, 1), (0, 3), (2, 0), (0, 2), (2, 2),
    (1, 1), (3, 3), (1, 3), (3, 1), (1, 2), (3, 2), (2, 1), (2, 3),
)
PLANE = len(OFFSETS)
SOURCES = (0, 1, 2, 7, 3, 4, 5, 6)
GROUPS = 2
NEAR = NZ // GROUPS
ROWS = 16
SOME = 2 * NEAR
WIDE = 4096
HALF = 384
TILE = 256
GO_WIDTHS = ((512, 1536, 2048), (1024, 1024, 1024, 1024))
BACK_WIDTHS = ((1024,3072),(1024,1024,1024,512,256,256))
STRAIGHT = 2
MESH = pl.DeviceIdType.MESH
F32 = jnp.float32
BF16 = jnp.bfloat16


def spans(widths):
    starts = [sum(widths[:c]) for c in range(len(widths))]
    return list(zip(starts, widths))


GO = tuple(spans(widths) for widths in GO_WIDTHS)
BACK = tuple(spans(widths) for widths in BACK_WIDTHS)
MOST_GO = max(len(widths) for widths in GO)
MOST_BACK = max(len(widths) for widths in BACK)


def dot(a, b):
    return jnp.dot(a, b, preferred_element_type=F32)


def kernel(
    tokens, routes_in, gates_in, placement_in, flags_in, w_gate, w_up, w_down, out,
    routes, gates, placement, flags, summed, in_sem, out_sem,
    tok, turned, meta, sel, comb_t, away, rows, w_in, w_out, acc, hid,
    mine, theirs, got, ret, back, part, hop_out, hop_in,
    w_sem, meta_send, meta_recv, ag_send, ag_recv, go_send, go_recv, sib_send, sib_recv,
    half_send, half_recv, back_send, back_recv, rs_send, rs_recv,
):
    dp = lax.axis_index("dp")
    ex = lax.axis_index("expert")
    x, core = dp // 2, dp % 2
    y, z = ex // NZ, ex % NZ
    sibling = (x * 2 + (1 - core), ex)

    def along_z(by):
        return (dp, y * NZ + (z + by * (1 - 2 * core) + NZ) % NZ)

    def in_plane(d, sign):
        dx, dy = OFFSETS[d]
        return (((x + sign * dx + NX) % NX) * 2 + core, ((y + sign * dy + NY) % NY) * NZ + z)

    def remote(src, dst, send, recv, device):
        return pltpu.make_async_remote_copy(
            src_ref=src, dst_ref=dst, send_sem=send, recv_sem=recv, device_id=device, device_id_type=MESH
        )

    barrier = pltpu.get_barrier_semaphore()
    for i in range(1, NZ):
        pl.semaphore_signal(barrier, inc=1, device_id=along_z(i), device_id_type=MESH)
    for d in range(1, PLANE):
        pl.semaphore_signal(barrier, inc=1, device_id=in_plane(d, 1), device_id_type=MESH)
    pl.semaphore_signal(barrier, inc=1, device_id=sibling, device_id_type=MESH)

    loads = (
        pltpu.make_async_copy(w_gate.at[0], w_in.at[:, pl.ds(0, HALF)], w_sem.at[0]),
        pltpu.make_async_copy(w_up.at[0], w_in.at[:, pl.ds(HALF, HALF)], w_sem.at[1]),
        pltpu.make_async_copy(w_down.at[0], w_out, w_sem.at[2]),
    )
    small = (
        pltpu.make_async_copy(routes_in, routes, in_sem.at[0]),
        pltpu.make_async_copy(gates_in, gates, in_sem.at[1]),
        pltpu.make_async_copy(placement_in, placement, in_sem.at[2]),
        pltpu.make_async_copy(flags_in, flags, in_sem.at[3]),
        pltpu.make_async_copy(tokens, tok.at[0], in_sem.at[4]),
    )
    for load in small + loads:
        load.start()
    for load in small:
        load.wait()

    turned[...] = jnp.zeros((128, 128), F32)
    turned[0:8, 0:ROWS] = routes[...].astype(F32)
    turned[8:16, 0:ROWS] = gates[...]
    meta[0] = turned[...].T[0:ROWS]

    pl.semaphore_wait(barrier, NZ - 1 + PLANE - 1 + 1)

    meta_copies = [
        remote(meta.at[0], meta.at[q], meta_send.at[q], meta_recv.at[q], along_z(-SOURCES[q])) for q in range(1, NZ)
    ]
    gather = {}

    def ag(g, c, q, src, by):
        cols = pl.ds(*GO[g][c])
        gather[(g, c, q)] = remote(
            src.at[:, cols], tok.at[q, :, cols], ag_send.at[c, q], ag_recv.at[c, q], along_z(by)
        )
        gather[(g, c, q)].start()

    for copy in meta_copies[:NEAR - 1]:
        copy.start()
    for c in range(len(GO[0])):
        for q in (2, 1, 3):
            ag(0, c, q, tok.at[0], -SOURCES[q])
        if c == 0:
            for copy in meta_copies[NEAR - 1:]:
                copy.start()

    def forward(c):
        ag(1, c, 5, tok.at[2], -2)
        ag(1, c, 6, tok.at[3], 2)
        ag(1, c, 4, tok.at[2], -1)
        ag(1, c, 7, tok.at[3], 1)

    lane = lax.broadcasted_iota(jnp.int32, (128, 128), 1)
    line = lax.broadcasted_iota(jnp.int32, (128, 128), 0)
    lane_f = lane.astype(F32)
    placed = jnp.broadcast_to(placement[...].astype(F32), (128, 128)).T
    flag = jnp.sum(
        jnp.where(placed == lane_f, jnp.broadcast_to(flags[...].astype(F32), (128, 128)), 0.0), axis=1, keepdims=True
    )
    holder = jnp.where(flag == 0.0, placed, jnp.where(placed >= 64.0, placed - 64.0, placed + 64.0))
    slot = lax.broadcasted_iota(jnp.int32, (8, 128), 1)
    far_x = jnp.zeros((8, 128), jnp.int32)
    far_y = jnp.zeros((8, 128), jnp.int32)
    for d, (dx, dy) in enumerate(OFFSETS):
        here = (slot & (PLANE - 1)) == d
        far_x = jnp.where(here, dx, far_x)
        far_y = jnp.where(here, dy, far_y)
    spot = (((far_y + y) & (NY - 1)) * NZ + z) * NX + ((far_x + x) & (NX - 1))
    spot = jnp.where(slot < 2 * PLANE, spot, -1).astype(F32)[0:1]
    where_to = jnp.where(holder == spot, 1.0, 0.0).astype(BF16)

    near_rows = NEAR * ROWS
    spot_row = lax.broadcasted_iota(jnp.int32, (SOME, near_rows), 0)
    ours = (lax.broadcasted_iota(jnp.int32, (SOME, near_rows), 1) >> 4) == (spot_row & (NEAR - 1))
    before_line = lax.broadcasted_iota(jnp.int32, (near_rows, near_rows), 0)
    before_lane = lax.broadcasted_iota(jnp.int32, (near_rows, near_rows), 1)
    before = jnp.where(
        ((before_line >> 4) == (before_lane >> 4)) & (before_lane < before_line), 1.0, 0.0
    ).astype(BF16)
    rank_lane = (lane[0:near_rows] >> 4).astype(F32)

    def spread(table):
        turned_table = table.T
        both = jnp.where(
            (spot_row >= NEAR)[None], turned_table[PLANE:2 * PLANE][:, None, :], turned_table[0:PLANE][:, None, :]
        )
        sel[...] = jnp.where(ours[None], both, 0.0)
        return sel[...].reshape(PLANE * SOME, near_rows)

    def picks(g):
        for q in range(max(1, g * NEAR), (g + 1) * NEAR):
            meta_copies[q - 1].wait_recv()
        info = meta[g * NEAR:(g + 1) * NEAR].reshape(near_rows, 128)
        named = jnp.zeros((near_rows, 128), F32)
        for k in range(8):
            named = named + jnp.where(info[:, k:k + 1] == lane_f[0:near_rows], 1.0, 0.0)
        at = dot(named.astype(BF16), where_to)
        rank = dot(before, at.astype(BF16))
        return info, jnp.where(rank == rank_lane, at, 0.0)

    tables = [picks(0)]
    chosen = [spread(tables[0][1]).astype(BF16)]

    def go(g, c, p):
        cols = pl.ds(*GO[g][c])
        return remote(
            away.at[g, p, :, cols], rows.at[g, 0, p, :, cols], go_send.at[g, c], go_recv.at[g, c], in_plane(p, 1)
        )

    others = pl.ds(1, PLANE - 1)

    def go_all(g, c):
        cols = pl.ds(*GO[g][c])
        return remote(
            away.at[g, others, :, cols], rows.at[g, 0, others, :, cols], go_send.at[g, c], go_recv.at[g, c], sibling
        )

    def dispatch(g, c):
        start, width = GO[g][c]
        for q in range(max(1, g * NEAR), (g + 1) * NEAR):
            gather[(g, c, q)].wait_recv()
        if g == 0:
            for far in range(len(GO[1])):
                if start < sum(GO[1][far]) <= start + width:
                    forward(far)
        for n in range(start, start + width, TILE):
            block = tok[g * NEAR:(g + 1) * NEAR, :, n:n + TILE].reshape(NEAR * ROWS, TILE)
            piece = dot(chosen[g], block).astype(BF16).reshape(PLANE, SOME, TILE)
            away[g, :, :, n:n + TILE] = piece
            rows[g, 0, 0, :, n:n + TILE] = piece[0]
        for p in range(1, PLANE):
            go(g, c, p).start()

    dispatch(0, 0)
    tables.append(picks(1))
    chosen.append(spread(tables[1][1]).astype(BF16))
    for c in range(1, len(GO[0])):
        dispatch(0, c)
    dispatch(1, 0)

    for g, (info, pick) in enumerate(tables):
        weight = jnp.zeros((near_rows, 128), F32)
        for k in range(8):
            weight = weight + jnp.where(info[:, k:k + 1] == lane_f[0:near_rows], info[:, 8 + k:9 + k], 0.0)
        high = weight.astype(BF16)
        low = (weight - high.astype(F32)).astype(BF16)
        for t, share_of in enumerate((high, low)):
            comb_t[g, t * 64:(t + 1) * 64] = spread(dot(share_of, where_to) * pick).T.astype(BF16)

    dispatch(1, 1)
    for load in loads:
        load.wait()

    def share(g, c):
        cols = pl.ds(*GO[g][c])
        return remote(rows.at[g, 0, :, :, cols], rows.at[g, 1, :, :, cols], sib_send.at[g, c], sib_recv.at[g, c], sibling)

    def first(g, c):
        start, width = GO[g][c]
        block = rows[g, :, :, :, start:start + width].reshape(2 * PLANE * SOME, width)
        for n in range(0, 2 * HALF, TILE):
            term = dot(block, w_in[start:start + width, n:n + TILE])
            if c == 0:
                acc[g, :, n:n + TILE] = term
            else:
                acc[g, :, n:n + TILE] += term

    def pair(g, c):
        cols = pl.ds(*BACK[g][c])
        return remote(theirs.at[g, :, cols], got.at[g, :, cols], half_send.at[g, c], half_recv.at[g, c], sibling)

    def home(g, c, p):
        cols = pl.ds(*BACK[g][c])
        return remote(
            ret.at[g, p, :, cols], back.at[g, p, :, cols], back_send.at[g, c], back_recv.at[g, c], in_plane(p, -1)
        )

    def home_all(g, c):
        cols = pl.ds(*BACK[g][c])
        return remote(
            ret.at[g, others, :, cols], back.at[g, others, :, cols], back_send.at[g, c], back_recv.at[g, c], sibling
        )

    def finish(g, c):
        start, width = BACK[g][c]
        cols = slice(start, start + width)
        pair(g, c).wait_recv()
        both = (mine[g, :, cols].astype(F32) + got[g, :, cols].astype(F32)).astype(BF16).reshape(PLANE, SOME, width)
        ret[g, :, :, cols] = both
        back[g, 0, :, cols] = both[0]
        for p in range(1, PLANE):
            home(g, c, p).start()

    def arrived(g, c):
        go_all(g, c).wait_recv()
        share(g, c).start()
        if c > 0:
            share(g, c - 1).wait_recv()
            first(g, c - 1)
        if c == len(GO[g]) - 1:
            share(g, c).wait_recv()
            first(g, c)

    def activate(g):
        gate_act = acc[g, :, 0:HALF]
        hid[g] = (gate_act / (1.0 + jnp.exp(-gate_act)) * acc[g, :, HALF:2 * HALF]).astype(BF16)

    def second(g, c):
        start, width = BACK[g][c]
        for n in range(start, start + width, TILE):
            two = dot(hid[g], w_out[:, n:n + TILE]).astype(BF16)
            mine[g, :, n:n + TILE] = two[0:128]
            theirs[g, :, n:n + TILE] = two[128:256]
        pair(g, c).start()

    def experts(g):
        activate(g)
        for c in range(len(BACK[g])):
            second(g, c)
            if c > 0:
                finish(g, c - 1)
        finish(g, len(BACK[g]) - 1)

    for c in range(len(GO[0])):
        if c == len(GO[0]) - 1:
            dispatch(1, 3)
        arrived(0, c)
        if c == 0:
            dispatch(1, 2)
    experts(0)
    for c in range(len(GO[1])):
        arrived(1, c)
    experts(1)

    def gathered(g, c):
        start, width = BACK[g][c]
        home_all(g, c).wait_recv()
        for n in range(start, start + width, TILE):
            block = back[g, :, :, n:n + TILE].reshape(PLANE * SOME, TILE)
            two = dot(comb_t[g], block)
            part[g * NEAR:(g + 1) * NEAR, :, n:n + TILE] = (two[0:64] + two[64:128]).reshape(NEAR, ROWS, TILE)

    ends = BACK[1]
    last = len(ends) - 1
    staged = len(ends) - STRAIGHT
    slot_of = {far: q for q, far in enumerate(SOURCES)}

    def rs(c, far, dst, by):
        cols = pl.ds(*ends[c])
        return remote(
            hop_out.at[far, :, cols], hop_in.at[dst, :, cols], rs_send.at[c, far], rs_recv.at[c, dst], along_z(by)
        )

    def rs_near(c):
        return rs(c, 1, 0, 1), rs(c, 7, 1, -1)

    def rs_far(c):
        if c >= staged:
            return tuple(rs(c, far, dst, far) for far, dst in ((4, 4), (3, 5), (5, 6), (6, 3), (2, 2)))
        return rs(c, 3, 4, 1), rs(c, 5, 5, -1), rs(c, 4, 6, 2)

    def rs_second(c):
        return () if c >= staged else (rs(c, 2, 2, 2), rs(c, 6, 3, -2))

    def leave(c, fars):
        start, width = ends[c]
        cols = slice(start, start + width)
        for far in fars:
            hop_out[far, :, cols] = part[slot_of[far], :, cols].astype(BF16)

    def middle(c):
        start, width = ends[c]
        cols = slice(start, start + width)
        for copy in rs_far(c):
            copy.wait_recv()
        up = part[slot_of[2], :, cols] + hop_in[4, :, cols].astype(F32) + hop_in[6, :, cols].astype(F32)
        down = part[slot_of[6], :, cols] + hop_in[5, :, cols].astype(F32)
        hop_out[2, :, cols] = up.astype(BF16)
        hop_out[6, :, cols] = down.astype(BF16)
        for copy in rs_second(c):
            copy.start()

    def written(c):
        cols = pl.ds(*ends[c])
        return pltpu.make_async_copy(summed.at[:, cols], out.at[:, cols], out_sem.at[c])

    def done(c):
        start, width = ends[c]
        cols = slice(start, start + width)
        for copy in rs_near(c) + (rs_far(c) if c >= staged else rs_second(c)):
            copy.wait_recv()
        total = part[0, :, cols]
        for i in range(NZ - 1 if c >= staged else 4):
            total = total + hop_in[i, :, cols].astype(F32)
        summed[:, cols] = total.astype(BF16)
        written(c).start()

    for c in range(len(BACK[0])):
        gathered(0, c)
    for c in range(last + 1):
        leave(c, (1, 7))
        for copy in rs_near(c):
            copy.start()
    for c in range(last + 1):
        gathered(1, c)
        leave(c, (4, 3, 5, 6, 2) if c >= staged else (3, 5, 4))
        for copy in rs_far(c):
            copy.start()
        if 0 < c < staged - 1:
            middle(c - 1)
        if c > 2 and c - 3 < staged - 2:
            done(c - 3)
    middle(staged - 2)
    for c in range(max(0, last - 2), staged - 2):
        done(c)
    middle(staged - 1)
    for c in range(staged, last):
        done(c)
    done(staged - 2)
    done(last)
    done(staged - 1)

    for copy in meta_copies:
        copy.wait_send()
    for copy in gather.values():
        copy.wait_send()
    for g in range(GROUPS):
        for c in range(len(GO[g])):
            go_all(g, c).wait_send()
            share(g, c).wait_send()
        for c in range(len(BACK[g])):
            pair(g, c).wait_send()
            home_all(g, c).wait_send()
    for c in range(last + 1):
        for copy in rs_near(c) + rs_far(c) + rs_second(c):
            copy.wait_send()
        written(c).wait()


def on_device(tokens, routes, route_gates, placement, swap_flags, gate_weight, up_weight, down_weight):
    hbm = pl.BlockSpec(memory_space=pl.ANY)
    dma = pltpu.SemaphoreType.DMA
    lanes = PLANE * SOME
    return pl.pallas_call(
        kernel,
        out_shape=jax.ShapeDtypeStruct(tokens.shape, tokens.dtype),
        in_specs=[hbm] * 8,
        out_specs=hbm,
        scratch_shapes=[
            pltpu.VMEM(routes.shape[::-1], jnp.int32),
            pltpu.VMEM(route_gates.shape[::-1], F32),
            pltpu.VMEM((1, 128), jnp.int32),
            pltpu.VMEM((1, 128), jnp.int32),
            pltpu.VMEM(tokens.shape, BF16),
            dma((5,)),
            dma((MOST_BACK,)),
            pltpu.VMEM((NZ, ROWS, WIDE), BF16),
            pltpu.VMEM((128, 128), F32),
            pltpu.VMEM((NZ, ROWS, 128), F32),
            pltpu.VMEM((PLANE, SOME, NEAR * ROWS), F32),
            pltpu.VMEM((GROUPS, 128, lanes), BF16),
            pltpu.VMEM((GROUPS, PLANE, SOME, WIDE), BF16),
            pltpu.VMEM((GROUPS, 2, PLANE, SOME, WIDE), BF16),
            pltpu.VMEM((WIDE, 2 * HALF), BF16),
            pltpu.VMEM((HALF, WIDE), BF16),
            pltpu.VMEM((GROUPS, 2 * lanes, 2 * HALF), F32),
            pltpu.VMEM((GROUPS, 2 * lanes, HALF), BF16),
            pltpu.VMEM((GROUPS, lanes, WIDE), BF16),
            pltpu.VMEM((GROUPS, lanes, WIDE), BF16),
            pltpu.VMEM((GROUPS, lanes, WIDE), BF16),
            pltpu.VMEM((GROUPS, PLANE, SOME, WIDE), BF16),
            pltpu.VMEM((GROUPS, PLANE, SOME, WIDE), BF16),
            pltpu.VMEM((NZ, ROWS, WIDE), F32),
            pltpu.VMEM((NZ, ROWS, WIDE), BF16),
            pltpu.VMEM((NZ - 1, ROWS, WIDE), BF16),
            dma((3,)),
            dma((NZ,)), dma((NZ,)),
            dma((MOST_GO, NZ)), dma((MOST_GO, NZ)),
            dma((GROUPS, MOST_GO)), dma((GROUPS, MOST_GO)),
            dma((GROUPS, MOST_GO)), dma((GROUPS, MOST_GO)),
            dma((GROUPS, MOST_BACK)), dma((GROUPS, MOST_BACK)),
            dma((GROUPS, MOST_BACK)), dma((GROUPS, MOST_BACK)),
            dma((MOST_BACK, NZ)), dma((MOST_BACK, NZ - 1)),
        ],
        compiler_params=pltpu.CompilerParams(
            collective_id=0, has_side_effects=True, vmem_limit_bytes=60 * 2**20
        ),
        name="moe",
    )(
        tokens, routes.T, route_gates.T, placement.reshape(1, -1), swap_flags.reshape(1, -1),
        gate_weight, up_weight, down_weight,
    )


def solution(mesh):
    return jax.shard_map(
        on_device,
        mesh=mesh,
        in_specs=(
            P(("dp", "expert"), None),
            P(("dp", "expert"), None),
            P(("dp", "expert"), None),
            P(),
            P(),
            P("expert", None, "dp"),
            P("expert", None, "dp"),
            P("expert", "dp", None),
        ),
        out_specs=P(("dp", "expert"), None),
        check_vma=False,
    )
```
